128 devices in a mesh: qrow: 8 (over z_lo, y), kcol: 16 (over z_hi, x, core).
Axes of the slice: x: 4, y: 4, z: 4 (z_hi: 2, z_lo: 2; z = z_hi * 2 + z_lo), core: 2. Of those that a mesh axis runs over, the one named last changes fastest.
Arguments:
- queries: bfloat16 [16384, 1024], P(('qrow', 'kcol')), may hold values from -100 to 100
- keys: bfloat16 [16384, 128], P(('qrow', 'kcol')), may hold values from -5 to 5
- values: bfloat16 [16384, 128], P(('qrow', 'kcol')), may hold values from -5 to 5
- query_feats: bfloat16 [16384, 512], P(('qrow', 'kcol')), may hold values from -5 to 5
- key_feats: bfloat16 [16384, 512], P(('qrow', 'kcol')), may hold values from -5 to 5
- block_pos: int32 [128], replicated, may hold values from 0 to 127, as said below
Outputs:
- query_grad: float32 [16384, 512], P(('qrow', 'kcol'))
- key_grad: float32 [16384, 512], P(('qrow', 'kcol'))
The draws below stay inside these ranges and needn't reach their ends.
Inputs may be any that keep to these rules, and one draw needn't show every extreme that they name: A permutation of the 128 sequence blocks: owner o holds block block_pos[o]; the owners 16 k to 16 k + 15 hold the blocks 16 k to 16 k + 15 in some order.
All inputs are finite; a program needn't handle non-finite values.
Results may differ from the reference program's by a relative error of at most 0.0022.
Values may be sent and summed in bfloat16 or wider, within the bound.
No kernel may reach another device: no remote copies, remote signals or barrier semaphores. Data moves between devices by JAX's collectives and lax.ppermute only.
A program may use at most 128 MiB of HBM per device.

```python
import math
import jax
import jax.numpy as jnp
from jax import lax

TOK_DEV = 128
HEADS = 8
HD = 128
FD = 64
TOKENS = 16384
N_KCOL = 16
DEVICES = 128


def shared_keys(key):
    base = jax.random.truncated_normal(jax.random.fold_in(key, 17), -5.0, 5.0, (DEVICES, TOK_DEV, HD), jnp.float32)
    return base


def draw_keys(key, part):
    return shared_keys(key).reshape(TOKENS, HD).astype(jnp.bfloat16)


def draw_queries(key, part):
    noise = jax.random.truncated_normal(jax.random.fold_in(key, 23), -5.0, 5.0, (DEVICES, TOK_DEV, HEADS, HD), jnp.float32)
    return noise.reshape(TOKENS, HEADS * HD).astype(jnp.bfloat16)


def draw_block_pos(key, part):
    groups = DEVICES // N_KCOL
    scores = jax.random.randint(jax.random.fold_in(key, 31), (groups, N_KCOL), 0, 1 << 20) * N_KCOL + jnp.arange(N_KCOL, dtype=jnp.int32)[None, :]
    order = jnp.argsort(scores, axis=1, stable=True).astype(jnp.int32)
    return (order + jnp.arange(groups, dtype=jnp.int32)[:, None] * N_KCOL).reshape(-1).astype(jnp.int32)


def level_of(key, dims, split, low, largest):
    factor_of, own = 1.0, jax.random.fold_in(key, 6)
    for axis_at, blocks in split:
        draws = jnp.exp(jax.random.uniform(jax.random.fold_in(own, axis_at), (blocks,), jnp.float32, low / len(split), largest / len(split)))
        factor_of = factor_of * jnp.repeat(draws, dims[axis_at] // blocks).reshape([-1 if axis == axis_at else 1 for axis in range(len(dims))])
    return factor_of


def scatter_about(key, dims, scale, reach, pieces=(), kind=jnp.bfloat16):
    result = jax.random.normal(key, dims, jnp.float32) * scale
    if len(pieces) > 0:
        result = level_of(key, dims, pieces, -0.22, 0.18) * result
    return jnp.clip(result, min=-reach, max=reach).astype(kind)


def setup_inputs(seed: int = 0) -> dict:
    arg_keys = jax.random.split(jax.random.key(seed), 7)
    queries = draw_queries(jax.random.fold_in(arg_keys[6], 71), 0)
    keys = draw_keys(jax.random.fold_in(arg_keys[6], 71), 0)
    values = scatter_about(arg_keys[2], (TOKENS, HD), 1.0, 5.0, ((0, 128),))
    query_feats = scatter_about(arg_keys[3], (TOKENS, HEADS * FD), 1.0, 5.0, ((0, 128),))
    key_feats = scatter_about(arg_keys[4], (TOKENS, HEADS * FD), 1.0, 5.0, ((0, 128),))
    block_pos = draw_block_pos(jax.random.fold_in(arg_keys[6], 71), 0)
    return {"queries": queries, "keys": keys, "values": values, "query_feats": query_feats, "key_feats": key_feats, "block_pos": block_pos}


FLOOR_SCORE = -1e+30

def contract_last(left, right):
    return lax.dot_general(left, right, (((1,), (1,)), ((), ())), preferred_element_type=jnp.float32)

def contract_first(left, right):
    return lax.dot_general(left, right, (((0,), (0,)), ((), ())), preferred_element_type=jnp.float32)

def reference(queries, keys, values, query_feats, key_feats, block_pos):
    seq_len = queries.shape[0]
    block_len = seq_len // block_pos.shape[0]
    head_size = keys.shape[1]
    head_count = queries.shape[1] // head_size
    feat_size = query_feats.shape[1] // head_count
    offsets = jnp.arange(block_len, dtype=jnp.int32)
    positions = (block_pos.astype(jnp.int32)[:, None] * block_len + offsets[None, :]).reshape(-1)
    counts = (positions + 1).astype(jnp.float32)
    row_block = block_len * N_KCOL
    block_count = seq_len // row_block
    key_scale = 1.0 / math.sqrt(head_size)
    feat_scale = 1.0 / math.sqrt(feat_size)
    q_heads = queries.reshape(seq_len, head_count, head_size).transpose(1, 0, 2)
    qf_heads = query_feats.reshape(seq_len, head_count, feat_size).transpose(1, 0, 2)
    kf_heads = key_feats.reshape(seq_len, head_count, feat_size).transpose(1, 0, 2)

    def one_head(operands):
        q_all, qf_all, kf_all = operands

        def step(key_acc, block_index):
            start = block_index * row_block
            q_rows = lax.dynamic_slice_in_dim(q_all, start, row_block, 0)
            qf_rows = lax.dynamic_slice_in_dim(qf_all, start, row_block, 0)
            pos_rows = lax.dynamic_slice_in_dim(positions, start, row_block, 0)
            cnt_rows = lax.dynamic_slice_in_dim(counts, start, row_block, 0)
            allowed = pos_rows[:, None] >= positions[None, :]
            scores = contract_last(q_rows, keys) * key_scale
            highest = lax.optimization_barrier(jnp.max(jnp.where(allowed, scores, FLOOR_SCORE), axis=1))
            totals = lax.optimization_barrier(jnp.sum(jnp.where(allowed, jnp.exp(scores - highest[:, None]), 0.0), axis=1))
            teacher = jnp.where(allowed, jnp.exp(scores - highest[:, None]), 0.0) / totals[:, None]
            student = jnp.where(allowed, contract_last(qf_rows, kf_all) * feat_scale / cnt_rows[:, None], 0.0)
            error = teacher - student
            mixed = jnp.dot(error.astype(jnp.bfloat16), values, preferred_element_type=jnp.float32).astype(jnp.bfloat16)
            coupled = contract_last(mixed, values) * key_scale
            weights = jnp.where(allowed, jnp.sqrt(cnt_rows)[:, None] * error + coupled, 0.0).astype(jnp.bfloat16)
            q_grad = -jnp.dot(weights, kf_all, preferred_element_type=jnp.float32)
            key_acc = key_acc - contract_first(weights, qf_rows)
            return (key_acc, q_grad)
        key_grad, q_blocks = lax.scan(step, jnp.zeros((seq_len, feat_size), jnp.float32), jnp.arange(block_count, dtype=jnp.int32))
        return (q_blocks.reshape(seq_len, feat_size), key_grad)
    q_grads, k_grads = lax.map(one_head, (q_heads, qf_heads, kf_heads))
    query_grad = q_grads.transpose(1, 0, 2).reshape(seq_len, head_count * feat_size)
    key_grad = k_grads.transpose(1, 0, 2).reshape(seq_len, head_count * feat_size)
    return (query_grad, key_grad)
```

```python
import math

import jax
import jax.numpy as jnp
from jax import lax
from jax.experimental import pallas as pl
from jax.experimental.pallas import tpu as pltpu
from jax.sharding import Mesh, PartitionSpec as P

FLOOR = -1e30
LOW = -1e29
F32 = jnp.float32
BF16 = jnp.bfloat16
HEADS = ("zl", "y")
COLS = ("zh", "x")
BLK = 128
GROUPS = 8
COLUMNS = 8
HD = 128
FD = 64
TR = 2 * BLK
TK = COLUMNS * BLK
VROWS = 208
KEY_SCALE = 1.0 / math.sqrt(HD)
FEAT_SCALE = 1.0 / math.sqrt(FD)
SCORE = KEY_SCALE * math.log2(math.e)


def nn(a, b):
    return lax.dot_general(a, b, (((1,), (0,)), ((), ())), preferred_element_type=F32)


def nt(a, b):
    return lax.dot_general(a, b, (((1,), (1,)), ((), ())), preferred_element_type=F32)


def tn(a, b):
    return lax.dot_general(a, b, (((0,), (0,)), ((), ())), preferred_element_type=F32)


def split(a):
    high = a.astype(BF16)
    return high, (a - high.astype(F32)).astype(BF16)


def iota(shape, dim):
    return lax.broadcasted_iota(jnp.int32, shape, dim)


def row_positions(rows_at, k):
    lane = iota((1, TR), 1)
    first = rows_at[2 * k] * BLK
    second = rows_at[2 * k + 1] * BLK - BLK
    return lane + jnp.where(lane < BLK, first, second)


def tile_mask(rows_at, keys_at, k):
    pos_rows = row_positions(rows_at, k)
    step = iota((BLK, 1), 0)
    parts = [pos_rows >= step + keys_at[COLUMNS * k + j] * BLK for j in range(COLUMNS)]
    return jnp.concatenate(parts, axis=0)


def load_rows(core, own, other, q_buf, qf_buf):
    for ref, slot in ((own, core[0]), (other, 1 - core[0])):
        at = pl.ds(pl.multiple_of(slot * BLK, BLK), BLK)
        for k in range(GROUPS):
            q_buf[k, at, :] = ref[k * BLK : (k + 1) * BLK, :]
            base = GROUPS * BLK + (k % 4) * BLK
            lanes = slice(0, FD) if k < 4 else slice(FD, 2 * FD)
            qf_buf[k, at, :] = ref[base : base + BLK, lanes]


def key_feats(slab, k):
    base = 2 * GROUPS * BLK + (k % 4) * BLK
    lanes = slice(0, FD) if k < 4 else slice(FD, 2 * FD)
    return slab[base : base + BLK, lanes]


def forward_kernel(rows_at, keys_at, core, own, other, *rest):
    slabs = rest[:COLUMNS]
    pack, okf, states, k_buf, kf_buf, vft, q_buf, qf_buf, acc, state = rest[COLUMNS:]
    load_rows(core, own, other, q_buf, qf_buf)
    for k in range(GROUPS):
        for j, slab in enumerate(slabs):
            at = slice(j * BLK, (j + 1) * BLK)
            feats = key_feats(slab, k)
            k_buf[k, at, :] = slab[k * BLK : (k + 1) * BLK, :]
            kf_buf[k, at, :] = feats
            v_at = GROUPS * BLK + k * BLK
            vft[k, :HD, at] = slab[v_at : v_at + BLK, :].T
            vft[k, HD : HD + FD, at] = feats.T
        tail = iota((VROWS - HD - FD, TK), 0)
        vft[k, HD + FD :, :] = jnp.where(tail == 0, 1.0, 0.0).astype(BF16)
    state[...] = jnp.zeros_like(state)

    def group(k, carry):
        acc[...] = jnp.zeros_like(acc)

        def add(kp, t, m):
            m_new = jnp.maximum(m, jnp.max(t, axis=0, keepdims=True))
            p = jnp.exp2(t - m_new).astype(BF16)
            acc[...] = acc[...] * jnp.exp2(m - m_new) + nn(vft[kp], p)
            return m_new

        def full(kp, m):
            return add(kp, nt(k_buf[kp], q_buf[k]) * SCORE, m)

        m = lax.fori_loop(0, k, full, jnp.full((1, TR), LOW, F32))
        mask = tile_mask(rows_at, keys_at, k)
        m = add(k, jnp.where(mask, nt(k_buf[k], q_buf[k]) * SCORE, FLOOR), m)
        inv_n = FEAT_SCALE / (row_positions(rows_at, k) + 1).astype(F32)
        student = jnp.where(mask, nt(kf_buf[k], qf_buf[k]) * inv_n, 0.0).astype(BF16)
        high, low = split(state[:HD, :])
        linear = nn(vft[k, :HD, :], student) + (nt(high, qf_buf[k]) + nt(low, qf_buf[k])) * inv_n
        pack[k, :HD, :] = acc[:HD, :]
        pack[k, HD : 2 * HD, :] = linear
        pack[k, 2 * HD :, :] = jnp.where(iota((8, TR), 0) == 0, acc[HD + FD : HD + FD + 1, :], m)
        okf[k] = acc[HD : HD + FD, :]
        states[k] = state[...]
        state[...] += nn(vft[k, : HD + FD, :], kf_buf[k])
        return carry

    lax.fori_loop(0, GROUPS, group, 0)


def backward_kernel(rows_at, keys_at, core, own, other, *rest):
    slabs = rest[:COLUMNS]
    mine, theirs, okf, states, dk_out, dq_out = rest[COLUMNS : COLUMNS + 6]
    k_buf, v_buf, kf_buf, kft, q_buf, qf_buf, r_buf, bias, acc, w_state, u_state = rest[COLUMNS + 6 :]
    load_rows(core, own, other, q_buf, qf_buf)
    for k in range(GROUPS):
        for j, slab in enumerate(slabs):
            at = slice(j * BLK, (j + 1) * BLK)
            feats = key_feats(slab, k)
            k_buf[k, at, :] = slab[k * BLK : (k + 1) * BLK, :]
            v_at = GROUPS * BLK + k * BLK
            v_buf[k, at, :] = slab[v_at : v_at + BLK, :]
            kf_buf[k, at, :] = feats
            kft[k, :, at] = feats.T

    def merge(k, carry):
        l0, m0 = mine[k, 2 * HD : 2 * HD + 1, :], mine[k, 2 * HD + 1 : 2 * HD + 2, :]
        l1, m1 = theirs[k, 2 * HD : 2 * HD + 1, :], theirs[k, 2 * HD + 1 : 2 * HD + 2, :]
        top = jnp.maximum(m0, m1)
        w0, w1 = jnp.exp2(m0 - top), jnp.exp2(m1 - top)
        total = l0 * w0 + l1 * w1
        w0, w1 = w0 / total, w1 / total
        mixed = (mine[k, :HD, :] * w0 + theirs[k, :HD, :] * w1) - (
            mine[k, HD : 2 * HD, :] + theirs[k, HD : 2 * HD, :]
        )
        r_buf[k] = mixed.astype(BF16)
        n = (row_positions(rows_at, k) + 1).astype(F32)
        bias[k] = 0.5 * jnp.log2(n) - (top + jnp.log2(total))
        dq_out[k] = okf[k] * (w0 * jnp.sqrt(n))
        return carry

    lax.fori_loop(0, GROUPS, merge, 0)
    w_state[...] = jnp.zeros_like(w_state)
    u_state[...] = jnp.zeros_like(u_state)

    def group(step, carry):
        kp = GROUPS - 1 - step
        w_high, w_low = split(w_state[...])
        u_high, u_low = split(u_state[...])
        v_tile, kf_tile = v_buf[kp], kf_buf[kp]
        acc[...] = (nn(v_tile, w_high) + nn(v_tile, w_low)) - (nn(kf_tile, u_high) + nn(kf_tile, u_low))

        def full(k, c):
            p = jnp.exp2(nt(k_buf[kp], q_buf[k]) * SCORE + bias[k]).astype(BF16)
            acc[...] += nn(p, qf_buf[k])
            return c

        lax.fori_loop(kp + 1, GROUPS, full, 0)
        mask = tile_mask(rows_at, keys_at, kp)
        n = (row_positions(rows_at, kp) + 1).astype(F32)
        weight = FEAT_SCALE / jnp.sqrt(n)
        r_tile, qf_tile = r_buf[kp], qf_buf[kp]
        teacher = jnp.where(mask, nt(k_buf[kp], q_buf[kp]) * SCORE + bias[kp], FLOOR)
        linear = nn(v_tile, r_tile) * KEY_SCALE - nt(kf_tile, qf_tile) * weight
        linear = jnp.where(mask, linear, 0.0)
        g = (jnp.exp2(teacher) + linear).astype(BF16)
        acc[...] += nn(g, qf_tile)
        s_high, s_low = split(states[kp])
        query = tn(s_high[:HD], r_tile) + tn(s_low[:HD], r_tile)
        student = nt(s_high[HD:], qf_tile) + nt(s_low[HD:], qf_tile)
        query = query * KEY_SCALE - student * weight + nn(kft[kp], linear.astype(BF16))
        dq_out[kp] = -(dq_out[kp] + query)
        w_state[...] += nn(r_tile, qf_tile) * KEY_SCALE
        f_high, f_low = split(qf_tile.astype(F32).T * weight)
        u_state[...] += nn(f_high, qf_tile) + nn(f_low, qf_tile)
        result = -acc[...]
        half = kp // 4
        row = pl.ds(pl.multiple_of((kp % 4) * BLK, BLK), BLK)

        @pl.when(half == 0)
        def _():
            for j in range(COLUMNS):
                dk_out[j, row, :FD] = result[j * BLK : (j + 1) * BLK, :]

        @pl.when(half == 1)
        def _():
            for j in range(COLUMNS):
                dk_out[j, row, FD:] = result[j * BLK : (j + 1) * BLK, :]

        return carry

    lax.fori_loop(0, GROUPS, group, 0)


def on_chip(count_smem, count_vmem):
    smem = [pl.BlockSpec(memory_space=pltpu.SMEM)] * count_smem
    return smem + [pl.BlockSpec(memory_space=pltpu.VMEM)] * count_vmem


def forward(rows_at, keys_at, core, own, other, slabs):
    return pl.pallas_call(
        forward_kernel,
        out_shape=(
            jax.ShapeDtypeStruct((GROUPS, 2 * HD + 8, TR), F32),
            jax.ShapeDtypeStruct((GROUPS, FD, TR), F32),
            jax.ShapeDtypeStruct((GROUPS, HD + FD, FD), F32),
        ),
        in_specs=on_chip(3, 2 + COLUMNS),
        out_specs=[pl.BlockSpec(memory_space=pltpu.VMEM)] * 3,
        scratch_shapes=[
            pltpu.VMEM((GROUPS, TK, HD), BF16),
            pltpu.VMEM((GROUPS, TK, FD), BF16),
            pltpu.VMEM((GROUPS, VROWS, TK), BF16),
            pltpu.VMEM((GROUPS, TR, HD), BF16),
            pltpu.VMEM((GROUPS, TR, FD), BF16),
            pltpu.VMEM((VROWS, TR), F32),
            pltpu.VMEM((HD + FD, FD), F32),
        ],
        name="forward",
    )(rows_at, keys_at, core, own, other, *slabs)


def backward(rows_at, keys_at, core, own, other, slabs, mine, theirs, okf, states):
    return pl.pallas_call(
        backward_kernel,
        out_shape=(
            jax.ShapeDtypeStruct((COLUMNS, 4 * BLK, 2 * FD), F32),
            jax.ShapeDtypeStruct((GROUPS, FD, TR), F32),
        ),
        in_specs=on_chip(3, 6 + COLUMNS),
        out_specs=[pl.BlockSpec(memory_space=pltpu.VMEM)] * 2,
        scratch_shapes=[
            pltpu.VMEM((GROUPS, TK, HD), BF16),
            pltpu.VMEM((GROUPS, TK, HD), BF16),
            pltpu.VMEM((GROUPS, TK, FD), BF16),
            pltpu.VMEM((GROUPS, FD, TK), BF16),
            pltpu.VMEM((GROUPS, TR, HD), BF16),
            pltpu.VMEM((GROUPS, TR, FD), BF16),
            pltpu.VMEM((GROUPS, HD, TR), BF16),
            pltpu.VMEM((GROUPS, 1, TR), F32),
            pltpu.VMEM((TK, FD), F32),
            pltpu.VMEM((HD, FD), F32),
            pltpu.VMEM((FD, FD), F32),
        ],
        name="backward",
    )(rows_at, keys_at, core, own, other, *slabs, mine, theirs, okf, states)


def shifted(a, step):
    return lax.ppermute(a, "x", [(i, (i + step) % 4) for i in range(4)])


def across(a, axis):
    return lax.ppermute(a, axis, [(0, 1), (1, 0)])


def pair_up(a):
    return jnp.concatenate([a[:4], a[4:]], axis=-1).reshape(4 * BLK, 2 * FD)


def per_device(queries, keys, values, query_feats, key_feats_in, block_pos):
    q_heads = queries.reshape(BLK, GROUPS, HD).transpose(1, 0, 2)
    feats = jnp.concatenate(
        [key_feats_in.reshape(BLK, GROUPS, FD), query_feats.reshape(BLK, GROUPS, FD)], axis=-1
    ).transpose(1, 0, 2)
    shared = jnp.broadcast_to(jnp.concatenate([keys, values], axis=0)[None], (GROUPS, 2 * BLK, HD))
    sent = jnp.concatenate([q_heads, shared, feats], axis=1)
    got = lax.all_to_all(sent, HEADS, 0, 0, tiled=True)
    own = jnp.concatenate([got[:, :BLK].reshape(-1, HD), pair_up(got[:, 3 * BLK :, FD:])], axis=0)
    slab = jnp.concatenate(
        [
            got[:, BLK : 2 * BLK].reshape(-1, HD),
            got[:, 2 * BLK : 3 * BLK].reshape(-1, HD),
            pair_up(got[:, 3 * BLK :, :FD]),
        ],
        axis=0,
    )
    other = across(own, "c")
    far = across(slab, "zh")
    left, right = shifted(slab, 1), shifted(slab, 3)
    far_left, far_right = shifted(far, 1), shifted(far, 3)
    half = slab.shape[0] // 2
    behind = jnp.concatenate([shifted(left[:half], 1), shifted(right[half:], 3)], axis=0)
    far_behind = jnp.concatenate([shifted(far_left[:half], 1), shifted(far_right[half:], 3)], axis=0)
    slabs = (slab, far, left, right, far_left, far_right, behind, far_behind)

    zh, x, c = lax.axis_index("zh"), lax.axis_index("x"), lax.axis_index("c")
    grid = block_pos.reshape(GROUPS, 2, 4, 2)
    fz = 1 - zh
    xl, xr, xb = (x + 3) % 4, (x + 1) % 4, (x + 2) % 4
    z_at = jnp.stack([zh, fz, zh, zh, fz, fz, zh, fz])
    x_at = jnp.stack([x, x, xl, xr, xl, xr, xb, xb])
    flat = grid.reshape(GROUPS, 16)
    keys_at = jnp.take(flat, z_at * 8 + x_at * 2 + c, axis=1).reshape(-1)
    rows_at = lax.dynamic_slice_in_dim(flat, zh * 8 + x * 2, 2, 1).reshape(-1)
    core = c.reshape(1).astype(jnp.int32)

    mine, okf, states = forward(rows_at, keys_at, core, own, other, slabs)
    theirs = across(mine, "c")
    dk, dq = backward(rows_at, keys_at, core, own, other, slabs, mine, theirs, okf, states)

    order = z_at * 4 + x_at
    dk = jnp.take(dk, jnp.argsort(order), axis=0)
    dk = lax.all_to_all(dk, COLS, 0, 0, tiled=True).sum(axis=0)
    dk = dk.reshape(4, BLK, 2, FD).transpose(2, 0, 1, 3).reshape(GROUPS, BLK, FD)
    dq = dq.reshape(GROUPS, FD, 2, BLK)
    keep = lax.dynamic_slice_in_dim(dq, c, 1, 2)
    give = lax.dynamic_slice_in_dim(dq, 1 - c, 1, 2)
    dq = (keep + across(give, "c"))[:, :, 0].transpose(0, 2, 1)
    final = lax.all_to_all(jnp.concatenate([dq, dk], axis=-1), HEADS, 0, 0, tiled=True)
    final = final.transpose(1, 0, 2)
    return final[:, :, :FD].reshape(BLK, -1), final[:, :, FD:].reshape(BLK, -1)


def solution(mesh):
    split_mesh = Mesh(mesh.devices.reshape(2, 4, 2, 4, 2), ("zl", "y", "zh", "x", "c"))
    spec = P(("zl", "y", "zh", "x", "c"), None)
    return jax.shard_map(
        per_device,
        mesh=split_mesh,
        in_specs=(spec,) * 5 + (P(),),
        out_specs=(spec, spec),
        check_vma=False,
    )
```

```python
import functools
import math

import jax
import jax.numpy as jnp
from jax import lax
from jax.experimental import pallas as pl
from jax.experimental.pallas import tpu as pltpu
from jax.sharding import Mesh, PartitionSpec as P

FLOOR = -1e30
LOW = -1e29
F32 = jnp.float32
BF16 = jnp.bfloat16
HEADS = ("zl", "y")
COLS = ("zh", "x")
BLK = 128
GROUPS = 8
COLUMNS = 8
HD = 128
FD = 64
TR = 2 * BLK
TK = COLUMNS * BLK
PAIRS = GROUPS // 2
VROWS = 208
ROW_L = VROWS
ROW_M = VROWS + HD
CARRY = ROW_M + 8
PACK = 2 * HD + 8
PLACES = ((0, 0), (1, 0), (0, 3), (0, 1), (1, 3), (1, 1), (0, 2), (1, 2))
KEY_SCALE = 1.0 / math.sqrt(HD)
FEAT_SCALE = 1.0 / math.sqrt(FD)
SCORE = KEY_SCALE * math.log2(math.e)


def nn(a, b):
    return lax.dot_general(a, b, (((1,), (0,)), ((), ())), preferred_element_type=F32)


def nt(a, b):
    return lax.dot_general(a, b, (((1,), (1,)), ((), ())), preferred_element_type=F32)


def tn(a, b):
    return lax.dot_general(a, b, (((0,), (0,)), ((), ())), preferred_element_type=F32)


def split(a):
    high = a.astype(BF16)
    return high, (a - high.astype(F32)).astype(BF16)


def iota(shape, dim):
    return lax.broadcasted_iota(jnp.int32, shape, dim)


def column(where, j):
    zh, x = PLACES[j]
    return (where[0] + zh) % 2, (where[1] + x) % 4


def row_positions(blocks, where, k):
    lane = iota((1, TR), 1)
    at = k * 16 + where[0] * 8 + where[1] * 2
    first = blocks[at] * BLK
    second = blocks[at + 1] * BLK - BLK
    return lane + jnp.where(lane < BLK, first, second)


def tile_mask(blocks, where, k, columns):
    pos_rows = row_positions(blocks, where, k)
    step = iota((BLK, 1), 0)
    parts = []
    for j in columns:
        zh, x = column(where, j)
        parts.append(pos_rows >= step + blocks[k * 16 + zh * 8 + x * 2 + where[2]] * BLK)
    return jnp.concatenate(parts, axis=0)


def block_at(base, k):
    return pl.ds(pl.multiple_of(base + k * BLK, BLK), BLK)


def load_rows(where, own, other, q_buf, qf_buf):
    for ref, slot in ((own, where[2]), (other, 1 - where[2])):
        at = pl.ds(pl.multiple_of(slot * BLK, BLK), BLK)
        for k in range(GROUPS):
            q_buf[k, at, :] = ref[k * BLK : (k + 1) * BLK, :]
            base = (GROUPS + k // 2) * BLK
            lanes = slice((k % 2) * FD, (k % 2 + 1) * FD)
            qf_buf[k, at, :] = ref[base : base + BLK, lanes]


def forward_kernel(columns, first, last, *refs):
    width = len(columns)
    keys_n = width * BLK
    blocks, where, own, other = refs[:4]
    slabs = refs[4 : 4 + width]
    refs = refs[4 + width :]
    if not first:
        carry_in, sums_in = refs[:2]
        refs = refs[2:]
    if last:
        pack, okf, states = refs[:3]
        carry, sums = refs[3:5]
        refs = refs[5:]
    else:
        carry, sums = refs[:2]
        refs = refs[2:]
    k_buf, kf_buf, vft, q_buf, qf_buf = refs
    load_rows(where, own, other, q_buf, qf_buf)
    if first:
        carry[...] = jnp.zeros_like(carry)
        for k in range(GROUPS):
            carry[k, ROW_M : ROW_M + 1, :] = jnp.full((1, TR), LOW, F32)
        sums[...] = jnp.zeros_like(sums)
    else:
        carry[...] = carry_in[...]
        sums[...] = sums_in[...]
    tail_rows = jnp.where(iota((VROWS - HD - FD, keys_n), 0) == 0, 1.0, 0.0).astype(BF16)
    for k in range(GROUPS):
        vft[k, HD + FD :, :] = tail_rows

    def update(rows, plans):
        olds = [carry[k, :VROWS, :] for k in rows]
        tops = [carry[k, ROW_M : ROW_M + 1, :] for k in rows]
        scores = []
        for k, plan in zip(rows, plans):
            found = []
            for g, mask in plan:
                s = nt(k_buf[g], q_buf[k])
                found.append(s if mask is None else jnp.where(mask, s, FLOOR))
            scores.append(found)
        results = []
        for old, top, found, plan in zip(olds, tops, scores, plans):
            new = top
            for s in found:
                new = jnp.maximum(new, jnp.max(s, axis=0, keepdims=True))
            total = old * jnp.exp2((top - new) * SCORE)
            for s, (g, _) in zip(found, plan):
                total = total + nn(vft[g], jnp.exp2((s - new) * SCORE).astype(BF16))
            results.append((total, new))
        for k, (total, new) in zip(rows, results):
            carry[k, :VROWS, :] = total
            carry[k, ROW_M : ROW_M + 1, :] = new

    def pair(i, c):
        a, b = 2 * i, 2 * i + 1
        step = 4 // width

        def full(u, c2):
            groups = [step * u + e for e in range(step)]
            update((a, b), [[(g, None) for g in groups]] * 2)
            return c2

        lax.fori_loop(0, i * 2 // step, full, 0)
        for j, slab in enumerate(slabs):
            at = slice(j * BLK, (j + 1) * BLK)
            feats = slab[block_at(2 * GROUPS * BLK, i), :]
            for e, k in enumerate((a, b)):
                part = feats[:, e * FD : (e + 1) * FD]
                k_buf[k, at, :] = slab[block_at(0, k), :]
                kf_buf[k, at, :] = part
                vft[k, :HD, at] = slab[block_at(GROUPS * BLK, k), :].T
                vft[k, HD : HD + FD, at] = part.T
        masks = [tile_mask(blocks, where, k, columns) for k in (a, b)]
        update((a, b), [[(a, masks[0])], [(a, None), (b, masks[1])]])
        for k, mask in zip((a, b), masks):
            inv_n = FEAT_SCALE / (row_positions(blocks, where, k) + 1).astype(F32)
            student = jnp.where(mask, nt(kf_buf[k], qf_buf[k]) * inv_n, 0.0).astype(BF16)
            carry[k, ROW_L:ROW_M, :] += nn(vft[k, :HD, :], student)
            sums[k] += nn(vft[k, : HD + FD, :], kf_buf[k])
        return c

    lax.fori_loop(0, PAIRS, pair, 0)
    if not last:
        return

    def finish(k, state):
        inv_n = FEAT_SCALE / (row_positions(blocks, where, k) + 1).astype(F32)
        high, low = split(state[:HD])
        linear = (nt(high, qf_buf[k]) + nt(low, qf_buf[k])) * inv_n
        pack[k, :HD, :] = carry[k, :HD, :]
        pack[k, HD : 2 * HD, :] = carry[k, ROW_L:ROW_M, :] + linear
        norm = carry[k, HD + FD : HD + FD + 1, :]
        top = carry[k, ROW_M : ROW_M + 1, :]
        pack[k, 2 * HD :, :] = jnp.where(iota((8, TR), 0) == 0, norm, top)
        okf[k] = carry[k, HD : HD + FD, :]
        states[k] = state
        return state + sums[k]

    state = jnp.zeros((HD + FD, FD), F32)
    for k in range(GROUPS):
        state = finish(k, state)


def backward_kernel(blocks, where, own, other, *rest):
    slabs = rest[:COLUMNS]
    mine, theirs, okf, states, dk_out, dq_out = rest[COLUMNS : COLUMNS + 6]
    k_buf, v_buf, kf_buf, kft, q_buf, qf_buf, r_buf, bias, acc, w_state, u_state = rest[COLUMNS + 6 :]
    load_rows(where, own, other, q_buf, qf_buf)

    for k in range(GROUPS):
        l0, m0 = mine[k, 2 * HD : 2 * HD + 1, :], mine[k, 2 * HD + 1 : 2 * HD + 2, :]
        l1, m1 = theirs[k, 2 * HD : 2 * HD + 1, :], theirs[k, 2 * HD + 1 : 2 * HD + 2, :]
        top = jnp.maximum(m0, m1)
        w0, w1 = jnp.exp2((m0 - top) * SCORE), jnp.exp2((m1 - top) * SCORE)
        total = l0 * w0 + l1 * w1
        w0, w1 = w0 / total, w1 / total
        mixed = (mine[k, :HD, :] * w0 + theirs[k, :HD, :] * w1) - (
            mine[k, HD : 2 * HD, :] + theirs[k, HD : 2 * HD, :]
        )
        r_buf[k] = mixed.astype(BF16)
        n = (row_positions(blocks, where, k) + 1).astype(F32)
        bias[k] = (0.5 * jnp.log2(n) - jnp.log2(total)) - top * SCORE
        dq_out[k] = okf[k] * (w0 * jnp.sqrt(n))
    w_state[...] = jnp.zeros_like(w_state)
    u_state[...] = jnp.zeros_like(u_state)

    def teach(g, k):
        return nt(k_buf[g], q_buf[k]) * SCORE + bias[k]

    def pair(step, c):
        i = PAIRS - 1 - step
        a, b = 2 * i, 2 * i + 1
        for j, slab in enumerate(slabs):
            at = slice(j * BLK, (j + 1) * BLK)
            feats = slab[block_at(2 * GROUPS * BLK, i), :]
            for e, g in enumerate((a, b)):
                part = feats[:, e * FD : (e + 1) * FD]
                k_buf[g, at, :] = slab[block_at(0, g), :]
                v_buf[g, at, :] = slab[block_at(GROUPS * BLK, g), :]
                kf_buf[g, at, :] = part
                kft[g, :, at] = part.T

        def diagonal(g, e):
            mask = tile_mask(blocks, where, g, range(COLUMNS))
            n = (row_positions(blocks, where, g) + 1).astype(F32)
            weight = FEAT_SCALE / jnp.sqrt(n)
            r_tile, qf_tile, v_tile, kf_tile = r_buf[g], qf_buf[g], v_buf[g], kf_buf[g]
            w_high, w_low = split(w_state[...])
            u_high, u_low = split(u_state[...])
            total = (nn(v_tile, w_high) + nn(v_tile, w_low)) - (nn(kf_tile, u_high) + nn(kf_tile, u_low))
            linear = nn(v_tile, r_tile) * KEY_SCALE - nt(kf_tile, qf_tile) * weight
            linear = jnp.where(mask, linear, 0.0)
            p = jnp.exp2(jnp.where(mask, teach(g, g), FLOOR))
            total = total + nn((p + linear).astype(BF16), qf_tile)
            if e == 0:
                p = jnp.exp2(teach(a, b)).astype(BF16)
                total = total + nn(p, qf_buf[b])
            acc[e] = total
            s_high, s_low = split(states[g])
            query = tn(s_high[:HD], r_tile) + tn(s_low[:HD], r_tile)
            student = nt(s_high[HD:], qf_tile) + nt(s_low[HD:], qf_tile)
            query = query * KEY_SCALE - student * weight + nn(kft[g], linear.astype(BF16))
            dq_out[g] = -(dq_out[g] + query)
            w_state[...] += nn(r_tile, qf_tile) * KEY_SCALE
            f_high, f_low = split(qf_tile.astype(F32).T * weight)
            u_state[...] += nn(f_high, qf_tile) + nn(f_low, qf_tile)

        diagonal(b, 1)
        diagonal(a, 0)

        def full(t, c2):
            olds = [acc[e] for e in range(2)]
            for e, g in enumerate((a, b)):
                for k in (2 * t, 2 * t + 1):
                    p = jnp.exp2(teach(g, k)).astype(BF16)
                    olds[e] = olds[e] + nn(p, qf_buf[k])
            for e in range(2):
                acc[e] = olds[e]
            return c2

        lax.fori_loop(i + 1, PAIRS, full, 0)
        for e in range(2):
            result = (-acc[e]).astype(dk_out.dtype)
            for j in range(COLUMNS):
                zh, x = column(where, j)
                dk_out[zh * 4 + x, block_at(0, i), e * FD : (e + 1) * FD] = result[j * BLK : (j + 1) * BLK, :]
        return c

    lax.fori_loop(0, PAIRS, pair, 0)


def on_chip(count_smem, count_vmem):
    smem = [pl.BlockSpec(memory_space=pltpu.SMEM)] * count_smem
    return smem + [pl.BlockSpec(memory_space=pltpu.VMEM)] * count_vmem


def forward(columns, blocks, where, own, other, slabs, carried, last):
    width = len(columns)
    carry = ((GROUPS, CARRY, TR), F32)
    sums = ((GROUPS, HD + FD, FD), F32)
    if last:
        outs = [((GROUPS, PACK, TR), F32), ((GROUPS, FD, TR), F32), sums]
        scratch = [pltpu.VMEM(*carry), pltpu.VMEM(*sums)]
    else:
        outs, scratch = [carry, sums], []
    scratch += [
        pltpu.VMEM((GROUPS, width * BLK, HD), BF16),
        pltpu.VMEM((GROUPS, width * BLK, FD), BF16),
        pltpu.VMEM((GROUPS, VROWS, width * BLK), BF16),
        pltpu.VMEM((GROUPS, TR, HD), BF16),
        pltpu.VMEM((GROUPS, TR, FD), BF16),
    ]
    return pl.pallas_call(
        functools.partial(forward_kernel, columns, not carried, last),
        out_shape=tuple(jax.ShapeDtypeStruct(*o) for o in outs),
        in_specs=on_chip(2, 2 + width + len(carried)),
        out_specs=[pl.BlockSpec(memory_space=pltpu.VMEM)] * len(outs),
        scratch_shapes=scratch,
        name="forward" + str(columns[0]),
    )(blocks, where, own, other, *[slabs[j] for j in columns], *carried)


def backward(blocks, where, own, other, slabs, mine, theirs, okf, states):
    return pl.pallas_call(
        backward_kernel,
        out_shape=(
            jax.ShapeDtypeStruct((COLUMNS, PAIRS * BLK, 2 * FD), BF16),
            jax.ShapeDtypeStruct((GROUPS, FD, TR), F32),
        ),
        in_specs=on_chip(2, 6 + COLUMNS),
        out_specs=[pl.BlockSpec(memory_space=pltpu.VMEM)] * 2,
        scratch_shapes=[
            pltpu.VMEM((GROUPS, TK, HD), BF16),
            pltpu.VMEM((GROUPS, TK, HD), BF16),
            pltpu.VMEM((GROUPS, TK, FD), BF16),
            pltpu.VMEM((GROUPS, FD, TK), BF16),
            pltpu.VMEM((GROUPS, TR, HD), BF16),
            pltpu.VMEM((GROUPS, TR, FD), BF16),
            pltpu.VMEM((GROUPS, HD, TR), BF16),
            pltpu.VMEM((GROUPS, 1, TR), F32),
            pltpu.VMEM((2, TK, FD), F32),
            pltpu.VMEM((HD, FD), F32),
            pltpu.VMEM((FD, FD), F32),
        ],
        name="backward",
    )(blocks, where, own, other, *slabs, mine, theirs, okf, states)


def shifted(a, step):
    return lax.ppermute(a, "x", [(i, (i + step) % 4) for i in range(4)])


def across(a, axis):
    return lax.ppermute(a, axis, [(0, 1), (1, 0)])


def pair_up(a):
    return a.reshape(PAIRS, 2, BLK, FD).transpose(0, 2, 1, 3).reshape(PAIRS * BLK, 2 * FD)


def per_device(queries, keys, values, query_feats, key_feats, block_pos):
    q_heads = queries.reshape(BLK, GROUPS, HD).transpose(1, 0, 2)
    feats = jnp.concatenate(
        [key_feats.reshape(BLK, GROUPS, FD), query_feats.reshape(BLK, GROUPS, FD)], axis=-1
    ).transpose(1, 0, 2)
    shared = jnp.broadcast_to(jnp.concatenate([keys, values], axis=0)[None], (GROUPS, 2 * BLK, HD))
    sent = jnp.concatenate([q_heads, shared, feats], axis=1)
    got = lax.all_to_all(sent, HEADS, 0, 0, tiled=True)
    slab = jnp.concatenate(
        [
            got[:, BLK : 2 * BLK].reshape(-1, HD),
            got[:, 2 * BLK : 3 * BLK].reshape(-1, HD),
            pair_up(got[:, 3 * BLK :, :FD]),
        ],
        axis=0,
    )
    own = jnp.concatenate([got[:, :BLK].reshape(-1, HD), pair_up(got[:, 3 * BLK :, FD:])], axis=0)
    far = across(slab, "zh")
    left, right = shifted(slab, 1), shifted(slab, 3)
    other = across(own, "c")
    far_left, far_right = shifted(far, 1), shifted(far, 3)
    half = slab.shape[0] // 2
    behind = jnp.concatenate([shifted(left[:half], 1), shifted(right[half:], 3)], axis=0)
    far_behind = jnp.concatenate([shifted(far_left[:half], 1), shifted(far_right[half:], 3)], axis=0)
    slabs = (slab, far, left, right, far_left, far_right, behind, far_behind)
    c = lax.axis_index("c")
    where = jnp.stack([lax.axis_index("zh"), lax.axis_index("x"), c]).astype(jnp.int32)

    carried = forward((0, 1), block_pos, where, own, other, slabs, (), False)
    carried = forward((2, 3, 4, 5), block_pos, where, own, other, slabs, carried, False)
    mine, okf, states = forward((6, 7), block_pos, where, own, other, slabs, carried, True)
    theirs = across(mine, "c")
    dk, dq = backward(block_pos, where, own, other, slabs, mine, theirs, okf, states)

    dk = lax.all_to_all(dk, COLS, 0, 0, tiled=True).astype(F32).sum(axis=0)
    dk = dk.reshape(PAIRS, BLK, 2, FD).transpose(0, 2, 1, 3).reshape(GROUPS, BLK, FD)
    dq = dq.reshape(GROUPS, FD, 2, BLK)
    keep = lax.dynamic_slice_in_dim(dq, c, 1, 2)
    give = lax.dynamic_slice_in_dim(dq, 1 - c, 1, 2)
    dq = (keep + across(give, "c"))[:, :, 0].transpose(0, 2, 1)
    final = lax.all_to_all(jnp.concatenate([dq, dk], axis=-1), HEADS, 0, 0, tiled=True)
    final = final.transpose(1, 0, 2)
    return final[:, :, :FD].reshape(BLK, -1), final[:, :, FD:].reshape(BLK, -1)


def solution(mesh):
    split_mesh = Mesh(mesh.devices.reshape(2, 4, 2, 4, 2), ("zl", "y", "zh", "x", "c"))
    spec = P(("zl", "y", "zh", "x", "c"), None)
    return jax.shard_map(
        per_device,
        mesh=split_mesh,
        in_specs=(spec,) * 5 + (P(),),
        out_specs=(spec, spec),
        check_vma=False,
    )
```

```python
import functools
import math

import jax
import jax.numpy as jnp
from jax import lax
from jax.experimental import pallas as pl
from jax.experimental.pallas import tpu as pltpu
from jax.sharding import Mesh, PartitionSpec as P

FLOOR = -1e30
LOW = -1e29
F32 = jnp.float32
BF16 = jnp.bfloat16
HEADS = ("zl", "y")
COLS = ("zh", "x")
BLK = 128
GROUPS = 8
COLUMNS = 8
HD = 128
FD = 64
TR = 2 * BLK
TK = COLUMNS * BLK
PAIRS = GROUPS // 2
HALF = BLK // 2
WIDTH = 2
KEYS = WIDTH * BLK
SLAB = 2 * BLK + HALF
ROWS = BLK + HALF
VROWS = 208
ROW_L = VROWS
ROW_M = VROWS + HD
CARRY = ROW_M + 8
PACK = 2 * HD + 8
PLACES = ((0, 0), (1, 0), (0, 3), (0, 1), (1, 3), (1, 1), (0, 2), (1, 2))
KEY_SCALE = 1.0 / math.sqrt(HD)
FEAT_SCALE = 1.0 / math.sqrt(FD)
SCORE = KEY_SCALE * math.log2(math.e)


def nn(a, b):
    return lax.dot_general(a, b, (((1,), (0,)), ((), ())), preferred_element_type=F32)


def nt(a, b):
    return lax.dot_general(a, b, (((1,), (1,)), ((), ())), preferred_element_type=F32)


def tn(a, b):
    return lax.dot_general(a, b, (((0,), (0,)), ((), ())), preferred_element_type=F32)


def split(a):
    high = a.astype(BF16)
    return high, (a - high.astype(F32)).astype(BF16)


def iota(shape, dim):
    return lax.broadcasted_iota(jnp.int32, shape, dim)


def column(where, j):
    zh, x = PLACES[j]
    return (where[0] + zh) % 2, (where[1] + x) % 4


def row_positions(blocks, where, k):
    lane = iota((1, TR), 1)
    at = k * 16 + where[0] * 8 + where[1] * 2
    first = blocks[at] * BLK
    second = blocks[at + 1] * BLK - BLK
    return lane + jnp.where(lane < BLK, first, second)


def tile_mask(blocks, where, k, columns):
    pos_rows = row_positions(blocks, where, k)
    step = iota((BLK, 1), 0)
    parts = []
    for j in columns:
        zh, x = column(where, j)
        parts.append(pos_rows >= step + blocks[k * 16 + zh * 8 + x * 2 + where[2]] * BLK)
    return jnp.concatenate(parts, axis=0)


def feats_of(ref, e, at):
    packed = ref[e, at : at + HALF, :]
    return packed[:, :FD], packed[:, FD:]


def core_slices(where):
    for mine, slot in ((True, where[2]), (False, 1 - where[2])):
        yield mine, pl.ds(pl.multiple_of(slot * BLK, BLK), BLK)


def forward_kernel(columns, first, last, *refs):
    blocks, where, own, other = refs[:4]
    slabs = refs[4 : 4 + WIDTH]
    refs = refs[4 + WIDTH :]
    if not first:
        carry_in, sums_in = refs[:2]
        refs = refs[2:]
    if last:
        pack, okf, states = refs[:3]
        carry, sums, prefix = refs[3:6]
        refs = refs[6:]
    else:
        carry, sums = refs[:2]
        refs = refs[2:]
    k_buf, kf_buf, vft, q_buf, qf_buf = refs
    i = pl.program_id(0)
    a, b = 2 * i, 2 * i + 1
    if last:

        @pl.when(i == 0)
        def _():
            prefix[...] = jnp.zeros_like(prefix)

    if first:
        carry[...] = jnp.zeros_like(carry)
        for e in range(2):
            carry[e, ROW_M : ROW_M + 1, :] = jnp.full((1, TR), LOW, F32)
        sums[...] = jnp.zeros_like(sums)
    else:
        carry[...] = carry_in[...]
        sums[...] = sums_in[...]
    for mine, at in core_slices(where):
        ref = own if mine else other
        for e in range(2):
            q_buf[e, at, :] = ref[e, :BLK, :]
            qf_buf[e, at, :] = jnp.concatenate(feats_of(ref, e, BLK), axis=0)

    def update(plans):
        olds = [carry[e, :VROWS, :] for e in range(2)]
        tops = [carry[e, ROW_M : ROW_M + 1, :] for e in range(2)]
        scores = []
        for e, plan in enumerate(plans):
            found = []
            for g, mask in plan:
                s = nt(k_buf[g], q_buf[e])
                found.append(s if mask is None else jnp.where(mask, s, FLOOR))
            scores.append(found)
        results = []
        for old, top, found, plan in zip(olds, tops, scores, plans):
            new = top
            for s in found:
                new = jnp.maximum(new, jnp.max(s, axis=0, keepdims=True))
            total = old * jnp.exp2((top - new) * SCORE)
            for s, (g, _) in zip(found, plan):
                total = total + nn(vft[g], jnp.exp2((s - new) * SCORE).astype(BF16))
            results.append((total, new))
        for e, (total, new) in enumerate(results):
            carry[e, :VROWS, :] = total
            carry[e, ROW_M : ROW_M + 1, :] = new

    def full(u, c):
        update([[(2 * u, None), (2 * u + 1, None)]] * 2)
        return c

    lax.fori_loop(0, i, full, 0)
    tail_rows = jnp.where(iota((VROWS - HD - FD, KEYS), 0) == 0, 1.0, 0.0).astype(BF16)
    for e, g in enumerate((a, b)):
        for j, slab in enumerate(slabs):
            at = slice(j * BLK, (j + 1) * BLK)
            feats = jnp.concatenate(feats_of(slab, e, 2 * BLK), axis=0)
            k_buf[g, at, :] = slab[e, :BLK, :]
            kf_buf[g, at, :] = feats
            vft[g, :HD, at] = slab[e, BLK : 2 * BLK, :].T
            vft[g, HD : HD + FD, at] = feats.T
        vft[g, HD + FD :, :] = tail_rows
    masks = [tile_mask(blocks, where, g, columns) for g in (a, b)]
    update([[(a, masks[0])], [(a, None), (b, masks[1])]])
    for e, (g, mask) in enumerate(zip((a, b), masks)):
        inv_n = FEAT_SCALE / (row_positions(blocks, where, g) + 1).astype(F32)
        student = jnp.where(mask, nt(kf_buf[g], qf_buf[e]) * inv_n, 0.0).astype(BF16)
        carry[e, ROW_L:ROW_M, :] += nn(vft[g, :HD, :], student)
        sums[e] += nn(vft[g, : HD + FD, :], kf_buf[g])
        if last:
            state = prefix[...]
            high, low = split(state[:HD])
            linear = (nt(high, qf_buf[e]) + nt(low, qf_buf[e])) * inv_n
            pack[e, :HD, :] = carry[e, :HD, :]
            pack[e, HD : 2 * HD, :] = carry[e, ROW_L:ROW_M, :] + linear
            norm = carry[e, HD + FD : HD + FD + 1, :]
            top = carry[e, ROW_M : ROW_M + 1, :]
            pack[e, 2 * HD :, :] = jnp.where(iota((8, TR), 0) == 0, norm, top)
            okf[e] = carry[e, HD : HD + FD, :]
            states[e] = state
            prefix[...] = state + sums[e]


def backward_kernel(blocks, where, own, other, *rest):
    slabs = rest[:COLUMNS]
    mine, theirs, okf, states, dk_out, dq_out = rest[COLUMNS : COLUMNS + 6]
    k_buf, v_buf, kf_buf, kft, q_buf, qf_buf, r_buf, bias, acc, w_state, u_state = rest[COLUMNS + 6 :]
    step = pl.program_id(0)
    i = PAIRS - 1 - step
    a, b = 2 * i, 2 * i + 1

    @pl.when(step == 0)
    def _():
        w_state[...] = jnp.zeros_like(w_state)
        u_state[...] = jnp.zeros_like(u_state)

    for here, at in core_slices(where):
        ref = own if here else other
        for e, k in enumerate((a, b)):
            q_buf[k, at, :] = ref[e, :BLK, :]
            qf_buf[k, :, at] = jnp.concatenate([part.T for part in feats_of(ref, e, BLK)], axis=1)
    for e, k in enumerate((a, b)):
        l0, m0 = mine[e, 2 * HD : 2 * HD + 1, :], mine[e, 2 * HD + 1 : 2 * HD + 2, :]
        l1, m1 = theirs[e, 2 * HD : 2 * HD + 1, :], theirs[e, 2 * HD + 1 : 2 * HD + 2, :]
        top = jnp.maximum(m0, m1)
        w0, w1 = jnp.exp2((m0 - top) * SCORE), jnp.exp2((m1 - top) * SCORE)
        total = l0 * w0 + l1 * w1
        w0, w1 = w0 / total, w1 / total
        mixed = (mine[e, :HD, :] * w0 + theirs[e, :HD, :] * w1) - (
            mine[e, HD : 2 * HD, :] + theirs[e, HD : 2 * HD, :]
        )
        r_buf[e] = mixed.astype(BF16)
        n = (row_positions(blocks, where, k) + 1).astype(F32)
        bias[k] = (0.5 * jnp.log2(n) - jnp.log2(total)) - top * SCORE
        dq_out[e] = okf[e] * (w0 * jnp.sqrt(n))
        for j, slab in enumerate(slabs):
            at = slice(j * BLK, (j + 1) * BLK)
            feats = jnp.concatenate(feats_of(slab, e, 2 * BLK), axis=0)
            k_buf[e, at, :] = slab[e, :BLK, :]
            v_buf[e, at, :] = slab[e, BLK : 2 * BLK, :]
            kf_buf[e, at, :] = feats
            kft[e, :, at] = feats.T

    def teach(e, k):
        return nt(k_buf[e], q_buf[k]) * SCORE + bias[k]

    def diagonal(g, e):
        mask = tile_mask(blocks, where, g, range(COLUMNS))
        n = (row_positions(blocks, where, g) + 1).astype(F32)
        weight = FEAT_SCALE / jnp.sqrt(n)
        r_tile, qf_tile, v_tile, kf_tile = r_buf[e], qf_buf[g], v_buf[e], kf_buf[e]
        w_high, w_low = split(w_state[...])
        u_high, u_low = split(u_state[...])
        total = (nt(w_high, v_tile) + nt(w_low, v_tile)) - (nt(u_high, kf_tile) + nt(u_low, kf_tile))
        linear = nn(v_tile, r_tile) * KEY_SCALE - nn(kf_tile, qf_tile) * weight
        linear = jnp.where(mask, linear, 0.0)
        p = jnp.exp2(jnp.where(mask, teach(e, g), FLOOR))
        total = total + nt(qf_tile, (p + linear).astype(BF16))
        if e == 0:
            p = jnp.exp2(teach(e, b)).astype(BF16)
            total = total + nt(qf_buf[b], p)
        acc[e] = total
        s_high, s_low = split(states[e])
        query = tn(s_high[:HD], r_tile) + tn(s_low[:HD], r_tile)
        student = nn(s_high[HD:], qf_tile) + nn(s_low[HD:], qf_tile)
        query = query * KEY_SCALE - student * weight + nn(kft[e], linear.astype(BF16))
        dq_out[e] = -(dq_out[e] + query)
        w_state[...] += nt(qf_tile, r_tile) * KEY_SCALE
        f_high, f_low = split(qf_tile.astype(F32) * weight)
        u_state[...] += nt(f_high, qf_tile) + nt(f_low, qf_tile)

    diagonal(b, 1)
    diagonal(a, 0)

    def full(t, c):
        olds = [acc[e] for e in range(2)]
        for e in range(2):
            p = [jnp.exp2(score).astype(BF16) for score in [teach(e, 2 * t), teach(e, 2 * t + 1)]]
            olds[e] = olds[e] + (nt(qf_buf[2 * t], p[0]) + nt(qf_buf[2 * t + 1], p[1]))
        for e in range(2):
            acc[e] = olds[e]
        return c

    lax.fori_loop(i + 1, PAIRS, full, 0)
    result = -jnp.concatenate([acc[0], acc[1]], axis=0).astype(dk_out.dtype)
    for j in range(COLUMNS):
        zh, x = column(where, j)
        dk_out[zh * 4 + x] = result[:, j * BLK : (j + 1) * BLK]


def smem(count):
    return [pl.BlockSpec(memory_space=pltpu.SMEM)] * count


def by_pair(rows, lanes, down=False):
    return pl.BlockSpec((2, rows, lanes), lambda s: (PAIRS - 1 - s if down else s, 0, 0))


def forward(columns, blocks, where, own, other, slabs, carried, last):
    carry = ((GROUPS, CARRY, TR), F32)
    sums = ((GROUPS, HD + FD, FD), F32)
    carry_specs = [by_pair(CARRY, TR), by_pair(HD + FD, FD)]
    if last:
        outs = [((GROUPS, PACK, TR), F32), ((GROUPS, FD, TR), F32), sums]
        out_specs = [by_pair(PACK, TR), by_pair(FD, TR), by_pair(HD + FD, FD)]
        scratch = [pltpu.VMEM((2, CARRY, TR), F32), pltpu.VMEM((2, HD + FD, FD), F32)]
        scratch += [pltpu.VMEM((HD + FD, FD), F32)]
    else:
        outs, out_specs, scratch = [carry, sums], carry_specs, []
    scratch += [
        pltpu.VMEM((GROUPS, KEYS, HD), BF16),
        pltpu.VMEM((GROUPS, KEYS, FD), BF16),
        pltpu.VMEM((GROUPS, VROWS, KEYS), BF16),
        pltpu.VMEM((2, TR, HD), BF16),
        pltpu.VMEM((2, TR, FD), BF16),
    ]
    in_specs = smem(2) + [by_pair(ROWS, HD)] * 2 + [by_pair(SLAB, HD)] * WIDTH
    return pl.pallas_call(
        functools.partial(forward_kernel, columns, not carried, last),
        grid=(PAIRS,),
        out_shape=tuple(jax.ShapeDtypeStruct(*o) for o in outs),
        in_specs=in_specs + (carry_specs if carried else []),
        out_specs=out_specs,
        scratch_shapes=scratch,
        cost_estimate=pl.CostEstimate(flops=6_000_000_000, transcendentals=2_400_000, bytes_accessed=8_000_000),
        name="forward" + str(columns[0]),
    )(blocks, where, own, other, *[slabs[j] for j in columns], *carried)


def backward(blocks, where, own, other, slabs, mine, theirs, okf, states):
    in_specs = smem(2) + [by_pair(ROWS, HD, True)] * 2 + [by_pair(SLAB, HD, True)] * COLUMNS
    in_specs += [by_pair(PACK, TR, True)] * 2 + [by_pair(FD, TR, True), by_pair(HD + FD, FD, True)]
    return pl.pallas_call(
        backward_kernel,
        grid=(PAIRS,),
        out_shape=(
            jax.ShapeDtypeStruct((COLUMNS, PAIRS * BLK, BLK), BF16),
            jax.ShapeDtypeStruct((GROUPS, FD, TR), F32),
        ),
        in_specs=in_specs,
        out_specs=[
            pl.BlockSpec((COLUMNS, BLK, BLK), lambda s: (0, PAIRS - 1 - s, 0)),
            by_pair(FD, TR, True),
        ],
        scratch_shapes=[
            pltpu.VMEM((2, TK, HD), BF16),
            pltpu.VMEM((2, TK, HD), BF16),
            pltpu.VMEM((2, TK, FD), BF16),
            pltpu.VMEM((2, FD, TK), BF16),
            pltpu.VMEM((GROUPS, TR, HD), BF16),
            pltpu.VMEM((GROUPS, FD, TR), BF16),
            pltpu.VMEM((2, HD, TR), BF16),
            pltpu.VMEM((GROUPS, 1, TR), F32),
            pltpu.VMEM((2, FD, TK), F32),
            pltpu.VMEM((FD, HD), F32),
            pltpu.VMEM((FD, FD), F32),
        ],
        cost_estimate=pl.CostEstimate(flops=20_000_000_000, transcendentals=9_400_000, bytes_accessed=16_000_000),
        name="backward",
    )(blocks, where, own, other, *slabs, mine, theirs, okf, states)


def shifted(a, step):
    return lax.ppermute(a, "x", [(i, (i + step) % 4) for i in range(4)])


def across(a, axis):
    return lax.ppermute(a, axis, [(0, 1), (1, 0)])


def by_head(feats):
    return feats.reshape(2, HALF, GROUPS, FD).transpose(2, 1, 0, 3).reshape(GROUPS, HALF, 2 * FD)


def per_device(queries, keys, values, query_feats, key_feats, block_pos):
    shared = jnp.broadcast_to(jnp.concatenate([keys, values], axis=0)[None], (GROUPS, 2 * BLK, HD))
    slab = lax.all_to_all(jnp.concatenate([shared, by_head(key_feats)], axis=1), HEADS, 0, 0, tiled=True)
    far = across(slab, "zh")
    left, right = shifted(slab, 1), shifted(slab, 3)
    q_heads = queries.reshape(BLK, GROUPS, HD).transpose(1, 0, 2)
    rows = jnp.concatenate([q_heads, by_head(query_feats)], axis=1)
    own = lax.all_to_all(rows, HEADS, 0, 0, tiled=True)
    other = across(own, "c")
    far_left, far_right = shifted(far, 1), shifted(far, 3)
    behind = jnp.concatenate([shifted(left[:4], 1), shifted(right[4:], 3)], axis=0)
    far_behind = jnp.concatenate([shifted(far_left[:4], 1), shifted(far_right[4:], 3)], axis=0)
    slabs = (slab, far, left, right, far_left, far_right, behind, far_behind)
    c = lax.axis_index("c")
    where = jnp.stack([lax.axis_index("zh"), lax.axis_index("x"), c]).astype(jnp.int32)

    carried = ()
    for first in range(0, COLUMNS, WIDTH):
        columns = tuple(range(first, first + WIDTH))
        carried = forward(columns, block_pos, where, own, other, slabs, carried, first + WIDTH == COLUMNS)
    mine, okf, states = carried
    theirs = across(mine, "c")
    dk, dq = backward(block_pos, where, own, other, slabs, mine, theirs, okf, states)

    dk = lax.all_to_all(dk, COLS, 0, 0, tiled=True).astype(F32).sum(axis=0)
    dk = dk.reshape(GROUPS, FD, BLK)
    dq = dq.reshape(GROUPS, FD, 2, BLK)
    keep = lax.dynamic_slice_in_dim(dq, c, 1, 2)
    give = lax.dynamic_slice_in_dim(dq, 1 - c, 1, 2)
    dq = (keep + across(give, "c"))[:, :, 0]
    final = lax.all_to_all(jnp.concatenate([dq, dk], axis=1), HEADS, 0, 0, tiled=True)
    dq, dk = final[:, :FD].reshape(-1, BLK), final[:, FD:].reshape(-1, BLK)
    return dq.T, dk.T


def solution(mesh):
    split_mesh = Mesh(mesh.devices.reshape(2, 4, 2, 4, 2), ("zl", "y", "zh", "x", "c"))
    spec = P(("zl", "y", "zh", "x", "c"), None)
    return jax.shard_map(
        per_device,
        mesh=split_mesh,
        in_specs=(spec,) * 5 + (P(),),
        out_specs=(spec, spec),
        check_vma=False,
    )
```

```python
import functools
import math

import jax
import jax.numpy as jnp
from jax import lax
from jax.experimental import pallas as pl
from jax.experimental.pallas import tpu as pltpu
from jax.sharding import Mesh, PartitionSpec as P

FLOOR = -1e30
LOW = -1e29
F32 = jnp.float32
BF16 = jnp.bfloat16
HEADS = ("zl", "y")
COLS = ("zh", "x")
BLK = 128
GROUPS = 8
COLUMNS = 8
HD = 128
FD = 64
TR = 2 * BLK
TK = COLUMNS * BLK
PAIRS = GROUPS // 2
HALF = BLK // 2
WIDTH = 4
KEYS = WIDTH * BLK
STEP = 4 // WIDTH
SLAB = 2 * BLK + HALF
ROWS = BLK + HALF
VROWS = 208
ROW_L = VROWS
ROW_M = VROWS + HD
CARRY = ROW_M + 8
PACK = 2 * HD + 8
PLACES = ((0, 0), (1, 0), (0, 3), (0, 1), (1, 3), (1, 1), (0, 2), (1, 2))
KEY_SCALE = 1.0 / math.sqrt(HD)
FEAT_SCALE = 1.0 / math.sqrt(FD)
SCORE = KEY_SCALE * math.log2(math.e)


def nn(a, b):
    return lax.dot_general(a, b, (((1,), (0,)), ((), ())), preferred_element_type=F32)


def nt(a, b):
    return lax.dot_general(a, b, (((1,), (1,)), ((), ())), preferred_element_type=F32)


def tn(a, b):
    return lax.dot_general(a, b, (((0,), (0,)), ((), ())), preferred_element_type=F32)


def split(a):
    high = a.astype(BF16)
    return high, (a - high.astype(F32)).astype(BF16)


def stacked(a):
    return jnp.concatenate(split(a), axis=0)


def halves(a):
    return a[: a.shape[0] // 2] + a[a.shape[0] // 2 :]


def iota(shape, dim):
    return lax.broadcasted_iota(jnp.int32, shape, dim)


def column(where, j):
    zh, x = PLACES[j]
    return (where[0] + zh) % 2, (where[1] + x) % 4


def row_positions(blocks, where, k):
    lane = iota((1, TR), 1)
    at = k * 16 + where[0] * 8 + where[1] * 2
    first = blocks[at] * BLK
    second = blocks[at + 1] * BLK - BLK
    return lane + jnp.where(lane < BLK, first, second)


def tile_mask(blocks, where, k, columns):
    pos_rows = row_positions(blocks, where, k)
    step = iota((BLK, 1), 0)
    parts = []
    for j in columns:
        zh, x = column(where, j)
        parts.append(pos_rows >= step + blocks[k * 16 + zh * 8 + x * 2 + where[2]] * BLK)
    return jnp.concatenate(parts, axis=0)


def feats_of(ref, e, at):
    packed = ref[e, at : at + HALF, :]
    return packed[:, :FD], packed[:, FD:]


def core_slices(where):
    for mine, slot in ((True, where[2]), (False, 1 - where[2])):
        yield mine, pl.ds(pl.multiple_of(slot * BLK, BLK), BLK)


def forward_kernel(columns, first, last, *refs):
    blocks, where, own, other = refs[:4]
    slabs = refs[4 : 4 + WIDTH]
    refs = refs[4 + WIDTH :]
    if not first:
        carry_in, sums_in = refs[:2]
        refs = refs[2:]
    if last:
        pack, okf, states = refs[:3]
        carry, sums, prefix = refs[3:6]
        refs = refs[6:]
    else:
        carry, sums = refs[:2]
        refs = refs[2:]
    k_buf, kf_buf, vft, q_buf, qf_buf = refs
    i = pl.program_id(0)
    a, b = 2 * i, 2 * i + 1
    if last:

        @pl.when(i == 0)
        def _():
            prefix[...] = jnp.zeros_like(prefix)

    if first:
        carry[...] = jnp.zeros_like(carry)
        for e in range(2):
            carry[e, ROW_M : ROW_M + 1, :] = jnp.full((1, TR), LOW, F32)
        sums[...] = jnp.zeros_like(sums)
    else:
        carry[...] = carry_in[...]
        sums[...] = sums_in[...]
    for mine, at in core_slices(where):
        ref = own if mine else other
        for e in range(2):
            q_buf[e, at, :] = ref[e, :BLK, :]
            qf_buf[e, at, :] = jnp.concatenate(feats_of(ref, e, BLK), axis=0)

    def update(plans):
        olds = [carry[e, :VROWS, :] for e in range(2)]
        tops = [carry[e, ROW_M : ROW_M + 1, :] for e in range(2)]
        scores = []
        for e, plan in enumerate(plans):
            found = []
            for g, mask in plan:
                for at in range(0, KEYS, TR):
                    s = nt(k_buf[g, at : at + TR, :], q_buf[e])
                    s = s if mask is None else jnp.where(mask[at : at + TR], s, FLOOR)
                    found.append((s, g, at))
            scores.append(found)
        results = []
        for old, top, found in zip(olds, tops, scores):
            new = top
            for s, _, _ in found:
                new = jnp.maximum(new, jnp.max(s, axis=0, keepdims=True))
            total = old * jnp.exp2((top - new) * SCORE)
            probs = [jnp.exp2((s - new) * SCORE).astype(BF16) for s, _, _ in found]
            for p, (_, g, at) in zip(probs, found):
                total = total + nn(vft[g, :, at : at + TR], p)
            results.append((total, new))
        for e, (total, new) in enumerate(results):
            carry[e, :VROWS, :] = total
            carry[e, ROW_M : ROW_M + 1, :] = new

    def full(u, c):
        update([[(STEP * u + e, None) for e in range(STEP)]] * 2)
        return c

    lax.fori_loop(0, 2 * i // STEP, full, 0)
    tail_rows = jnp.where(iota((VROWS - HD - FD, KEYS), 0) == 0, 1.0, 0.0).astype(BF16)
    for e, g in enumerate((a, b)):
        for j, slab in enumerate(slabs):
            at = slice(j * BLK, (j + 1) * BLK)
            feats = jnp.concatenate(feats_of(slab, e, 2 * BLK), axis=0)
            k_buf[g, at, :] = slab[e, :BLK, :]
            kf_buf[g, at, :] = feats
            vft[g, :HD, at] = slab[e, BLK : 2 * BLK, :].T
            vft[g, HD : HD + FD, at] = feats.T
        vft[g, HD + FD :, :] = tail_rows
    masks = [tile_mask(blocks, where, g, columns) for g in (a, b)]
    update([[(a, masks[0])], [(a, None), (b, masks[1])]])
    for e, (g, mask) in enumerate(zip((a, b), masks)):
        inv_n = FEAT_SCALE / (row_positions(blocks, where, g) + 1).astype(F32)
        student = jnp.where(mask, nt(kf_buf[g], qf_buf[e]) * inv_n, 0.0).astype(BF16)
        carry[e, ROW_L:ROW_M, :] += nn(vft[g, :HD, :], student)
        sums[e] += nn(vft[g, : HD + FD, :], kf_buf[g])
        if last:
            state = prefix[...]
            high, low = split(state[:HD])
            linear = (nt(high, qf_buf[e]) + nt(low, qf_buf[e])) * inv_n
            pack[e, :HD, :] = carry[e, :HD, :]
            pack[e, HD : 2 * HD, :] = carry[e, ROW_L:ROW_M, :] + linear
            norm = carry[e, HD + FD : HD + FD + 1, :]
            top = carry[e, ROW_M : ROW_M + 1, :]
            pack[e, 2 * HD :, :] = jnp.where(iota((8, TR), 0) == 0, norm, top)
            okf[e] = carry[e, HD : HD + FD, :]
            states[e] = state.T
            prefix[...] = state + sums[e]


def backward_kernel(blocks, where, own, other, *rest):
    slabs = rest[:COLUMNS]
    mine, theirs, okf, states, dk_out, dq_out = rest[COLUMNS : COLUMNS + 6]
    k_buf, vk_buf, kft, q_buf, qf_buf, rk_buf, bias, acc, state = rest[COLUMNS + 6 :]
    step = pl.program_id(0)
    i = PAIRS - 1 - step
    a, b = 2 * i, 2 * i + 1

    @pl.when(step == 0)
    def _():
        state[...] = jnp.zeros_like(state)

    for here, at in core_slices(where):
        ref = own if here else other
        for e, k in enumerate((a, b)):
            q_buf[k, at, :] = ref[e, :BLK, :]
            qf_buf[k, :, at] = jnp.concatenate([part.T for part in feats_of(ref, e, BLK)], axis=1)
    for e, k in enumerate((a, b)):
        l0, m0 = mine[e, 2 * HD : 2 * HD + 1, :], mine[e, 2 * HD + 1 : 2 * HD + 2, :]
        l1, m1 = theirs[e, 2 * HD : 2 * HD + 1, :], theirs[e, 2 * HD + 1 : 2 * HD + 2, :]
        top = jnp.maximum(m0, m1)
        w0, w1 = jnp.exp2((m0 - top) * SCORE), jnp.exp2((m1 - top) * SCORE)
        total = l0 * w0 + l1 * w1
        w0, w1 = w0 / total, w1 / total
        mixed = (mine[e, :HD, :] * w0 + theirs[e, :HD, :] * w1) - (
            mine[e, HD : 2 * HD, :] + theirs[e, HD : 2 * HD, :]
        )
        n = (row_positions(blocks, where, k) + 1).astype(F32)
        student = split(qf_buf[k].astype(F32) * (-FEAT_SCALE / (KEY_SCALE * jnp.sqrt(n))))
        rk_buf[e] = jnp.concatenate([mixed.astype(BF16), *student], axis=0)
        bias[k] = (0.5 * jnp.log2(n) - jnp.log2(total)) - top * SCORE
        dq_out[e] = okf[e] * (w0 * jnp.sqrt(n))
        for j, slab in enumerate(slabs):
            at = slice(j * BLK, (j + 1) * BLK)
            feats = jnp.concatenate(feats_of(slab, e, 2 * BLK), axis=0)
            k_buf[e, at, :] = slab[e, :BLK, :]
            vk_buf[e, at, :] = jnp.concatenate([slab[e, BLK : 2 * BLK, :], feats, feats], axis=1)
            kft[e, :, at] = feats.T

    def teach(e, k):
        return nt(k_buf[e], q_buf[k]) * SCORE + bias[k]

    def diagonal(g, e):
        mask = tile_mask(blocks, where, g, range(COLUMNS))
        rk_tile, qf_tile, vk_tile = rk_buf[e], qf_buf[g], vk_buf[e]
        linear = jnp.where(mask, nn(vk_tile, rk_tile) * KEY_SCALE, 0.0)
        p = jnp.exp2(jnp.where(mask, teach(e, g), FLOOR))
        total = halves(nt(stacked(state[...]), vk_tile)) * KEY_SCALE
        total = total + nt(qf_tile, (p + linear).astype(BF16))
        if e == 0:
            p = jnp.exp2(teach(e, b)).astype(BF16)
            total = total + nt(qf_buf[b], p)
        acc[e] = total
        past = states[e]
        query = halves(nn(stacked(jnp.concatenate([past, past[:, HD:]], axis=1)), rk_tile)) * KEY_SCALE
        query = query + nn(kft[e], linear.astype(BF16))
        dq_out[e] = -(dq_out[e] + query)
        state[...] += nt(qf_tile, rk_tile)

    diagonal(b, 1)
    diagonal(a, 0)

    def full(t, c):
        olds = [acc[e] for e in range(2)]
        for e in range(2):
            p = [jnp.exp2(score).astype(BF16) for score in [teach(e, 2 * t), teach(e, 2 * t + 1)]]
            olds[e] = olds[e] + (nt(qf_buf[2 * t], p[0]) + nt(qf_buf[2 * t + 1], p[1]))
        for e in range(2):
            acc[e] = olds[e]
        return c

    lax.fori_loop(i + 1, PAIRS, full, 0)
    result = -jnp.concatenate([acc[0], acc[1]], axis=0).astype(dk_out.dtype)
    for j in range(COLUMNS):
        zh, x = column(where, j)
        dk_out[zh * 4 + x] = result[:, j * BLK : (j + 1) * BLK]


def smem(count):
    return [pl.BlockSpec(memory_space=pltpu.SMEM)] * count


def by_pair(rows, lanes, down=False):
    return pl.BlockSpec((2, rows, lanes), lambda s: (PAIRS - 1 - s if down else s, 0, 0))


def forward(columns, blocks, where, own, other, slabs, carried, last):
    carry = ((GROUPS, CARRY, TR), F32)
    sums = ((GROUPS, HD + FD, FD), F32)
    carry_specs = [by_pair(CARRY, TR), by_pair(HD + FD, FD)]
    if last:
        outs = [((GROUPS, PACK, TR), F32), ((GROUPS, FD, TR), F32), ((GROUPS, FD, HD + FD), F32)]
        out_specs = [by_pair(PACK, TR), by_pair(FD, TR), by_pair(FD, HD + FD)]
        scratch = [pltpu.VMEM((2, CARRY, TR), F32), pltpu.VMEM((2, HD + FD, FD), F32)]
        scratch += [pltpu.VMEM((HD + FD, FD), F32)]
    else:
        outs, out_specs, scratch = [carry, sums], carry_specs, []
    scratch += [
        pltpu.VMEM((GROUPS, KEYS, HD), BF16),
        pltpu.VMEM((GROUPS, KEYS, FD), BF16),
        pltpu.VMEM((GROUPS, VROWS, KEYS), BF16),
        pltpu.VMEM((2, TR, HD), BF16),
        pltpu.VMEM((2, TR, FD), BF16),
    ]
    in_specs = smem(2) + [by_pair(ROWS, HD)] * 2 + [by_pair(SLAB, HD)] * WIDTH
    return pl.pallas_call(
        functools.partial(forward_kernel, columns, not carried, last),
        grid=(PAIRS,),
        out_shape=tuple(jax.ShapeDtypeStruct(*o) for o in outs),
        in_specs=in_specs + (carry_specs if carried else []),
        out_specs=out_specs,
        scratch_shapes=scratch,
        cost_estimate=pl.CostEstimate(flops=6_000_000_000, transcendentals=2_400_000, bytes_accessed=8_000_000),
        name="forward" + str(columns[0]),
    )(blocks, where, own, other, *slabs, *carried)


def backward(blocks, where, own, other, slabs, mine, theirs, okf, states):
    in_specs = smem(2) + [by_pair(ROWS, HD, True)] * 2 + [by_pair(SLAB, HD, True)] * COLUMNS
    in_specs += [by_pair(PACK, TR, True)] * 2 + [by_pair(FD, TR, True), by_pair(FD, HD + FD, True)]
    return pl.pallas_call(
        backward_kernel,
        grid=(PAIRS,),
        out_shape=(
            jax.ShapeDtypeStruct((COLUMNS, PAIRS * BLK, BLK), BF16),
            jax.ShapeDtypeStruct((GROUPS, FD, TR), F32),
        ),
        in_specs=in_specs,
        out_specs=[
            pl.BlockSpec((COLUMNS, BLK, BLK), lambda s: (0, PAIRS - 1 - s, 0)),
            by_pair(FD, TR, True),
        ],
        scratch_shapes=[
            pltpu.VMEM((2, TK, HD), BF16),
            pltpu.VMEM((2, TK, TR), BF16),
            pltpu.VMEM((2, FD, TK), BF16),
            pltpu.VMEM((GROUPS, TR, HD), BF16),
            pltpu.VMEM((GROUPS, FD, TR), BF16),
            pltpu.VMEM((2, TR, TR), BF16),
            pltpu.VMEM((GROUPS, 1, TR), F32),
            pltpu.VMEM((2, FD, TK), F32),
            pltpu.VMEM((FD, TR), F32),
        ],
        cost_estimate=pl.CostEstimate(flops=20_000_000_000, transcendentals=9_400_000, bytes_accessed=16_000_000),
        name="backward",
    )(blocks, where, own, other, *slabs, mine, theirs, okf, states)


def shifted(a, step):
    return lax.ppermute(a, "x", [(i, (i + step) % 4) for i in range(4)])


def across(a, axis):
    return lax.ppermute(a, axis, [(0, 1), (1, 0)])


def by_head(feats):
    return feats.reshape(2, HALF, GROUPS, FD).transpose(2, 1, 0, 3).reshape(GROUPS, HALF, 2 * FD)


def per_device(queries, keys, values, query_feats, key_feats, block_pos):
    shared = jnp.broadcast_to(jnp.concatenate([keys, values], axis=0)[None], (GROUPS, 2 * BLK, HD))
    slab = lax.all_to_all(jnp.concatenate([shared, by_head(key_feats)], axis=1), HEADS, 0, 0, tiled=True)
    far = across(slab, "zh")
    left, right = shifted(slab, 1), shifted(slab, 3)
    q_heads = queries.reshape(BLK, GROUPS, HD).transpose(1, 0, 2)
    rows = jnp.concatenate([q_heads, by_head(query_feats)], axis=1)
    own = lax.all_to_all(rows, HEADS, 0, 0, tiled=True)
    other = across(own, "c")
    far_left, far_right = shifted(far, 1), shifted(far, 3)
    behind = jnp.concatenate([shifted(left[:4], 1), shifted(right[4:], 3)], axis=0)
    c = lax.axis_index("c")
    where = jnp.stack([lax.axis_index("zh"), lax.axis_index("x"), c]).astype(jnp.int32)

    carried = forward((0, 1, 2, 3), block_pos, where, own, other, (slab, far, left, right), (), False)
    far_left, far_right, *carried = lax.optimization_barrier((far_left, far_right, *carried))
    far_behind = jnp.concatenate([shifted(far_left[:4], 1), shifted(far_right[4:], 3)], axis=0)
    slabs = (slab, far, left, right, far_left, far_right, behind, far_behind)
    mine, okf, states = forward((4, 5, 6, 7), block_pos, where, own, other, slabs[4:], carried, True)
    theirs = across(mine, "c")
    dk, dq = backward(block_pos, where, own, other, slabs, mine, theirs, okf, states)

    dk = lax.all_to_all(dk, COLS, 0, 0, tiled=True).astype(F32).sum(axis=0)
    dq = dq.reshape(GROUPS, FD, 2, BLK)
    keep = lax.dynamic_slice_in_dim(dq, c, 1, 2)
    give = lax.dynamic_slice_in_dim(dq, 1 - c, 1, 2)
    dq = (keep + across(give, "c"))[:, :, 0]
    final = jnp.concatenate([dq, dk.reshape(GROUPS, FD, BLK)], axis=1)
    final = lax.all_to_all(final, HEADS, 0, 0, tiled=True)
    return final[:, :FD].reshape(-1, BLK).T, final[:, FD:].reshape(-1, BLK).T


def solution(mesh):
    split_mesh = Mesh(mesh.devices.reshape(2, 4, 2, 4, 2), ("zl", "y", "zh", "x", "c"))
    spec = P(("zl", "y", "zh", "x", "c"), None)
    return jax.shard_map(
        per_device,
        mesh=split_mesh,
        in_specs=(spec,) * 5 + (P(),),
        out_specs=(spec, spec),
        check_vma=False,
    )
```

```python
import math

import jax
import jax.numpy as jnp
from jax import lax
from jax.experimental import pallas as pl
from jax.experimental.pallas import tpu as pltpu
from jax.sharding import Mesh, PartitionSpec as P

FLOOR = -1e30
LOW = -1e29
F32 = jnp.float32
BF16 = jnp.bfloat16
HEADS = ("zl", "y")
COLS = ("zh", "x")
BLK = 128
GROUPS = 8
COLUMNS = 8
HD = 128
FD = 64
TR = 2 * BLK
TK = COLUMNS * BLK
PAIRS = GROUPS // 2
HALF = BLK // 2
PART = BLK + HALF
SAFE = 2.0**100
VROWS = 208
PACK = 2 * HD + 8
PLACES = ((0, 0), (1, 0), (0, 3), (0, 1), (1, 3), (1, 1), (0, 2), (1, 2))
KEY_SCALE = 1.0 / math.sqrt(HD)
FEAT_SCALE = 1.0 / math.sqrt(FD)
SCORE = KEY_SCALE * math.log2(math.e)


def nn(a, b):
    return lax.dot_general(a, b, (((1,), (0,)), ((), ())), preferred_element_type=F32)


def nt(a, b):
    return lax.dot_general(a, b, (((1,), (1,)), ((), ())), preferred_element_type=F32)


def tn(a, b):
    return lax.dot_general(a, b, (((0,), (0,)), ((), ())), preferred_element_type=F32)


def split(a):
    high = a.astype(BF16)
    return high, (a - high.astype(F32)).astype(BF16)


def stacked(a):
    return jnp.concatenate(split(a), axis=0)


def halves(a):
    return a[: a.shape[0] // 2] + a[a.shape[0] // 2 :]


def iota(shape, dim):
    return lax.broadcasted_iota(jnp.int32, shape, dim)


def column(where, j):
    zh, x = PLACES[j]
    return (where[0] + zh) % 2, (where[1] + x) % 4


def row_positions(blocks, where, k):
    lane = iota((1, TR), 1)
    at = k * 16 + where[0] * 8 + where[1] * 2
    first = blocks[at] * BLK
    second = blocks[at + 1] * BLK - BLK
    return lane + jnp.where(lane < BLK, first, second)


def tile_mask(blocks, where, k, columns):
    pos_rows = row_positions(blocks, where, k)
    step = iota((BLK, 1), 0)
    parts = []
    for j in columns:
        zh, x = column(where, j)
        parts.append(pos_rows >= step + blocks[k * 16 + zh * 8 + x * 2 + where[2]] * BLK)
    return jnp.concatenate(parts, axis=0)


def feats_of(ref, e, at):
    packed = ref[e, at : at + HALF, :]
    return packed[:, :FD], packed[:, FD:]


def core_slices(where):
    for mine, slot in ((True, where[2]), (False, 1 - where[2])):
        yield mine, pl.ds(pl.multiple_of(slot * BLK, BLK), BLK)


def forward_kernel(blocks, where, own, other, values, *refs):
    slabs = refs[:COLUMNS]
    pack, okf, states, k_buf, vft, q_buf, qf_buf, sums, tops, prefix = refs[COLUMNS:]
    i = pl.program_id(0)
    a, b = 2 * i, 2 * i + 1

    @pl.when(i == 0)
    def _():
        prefix[...] = jnp.zeros_like(prefix)

    for mine, at in core_slices(where):
        ref = own if mine else other
        for e in range(2):
            q_buf[e, at, :] = ref[e, :BLK, :]
            qf_buf[e, at, :] = jnp.concatenate(feats_of(ref, e, BLK), axis=0)

    def scores_of(e, g, mask=None):
        found = []
        for at in range(0, TK, TR):
            s = nt(k_buf[g, at : at + TR, :], q_buf[e])
            found.append(s if mask is None else jnp.where(mask[at : at + TR], s, FLOOR))
        return found

    def mixed(g, found, top):
        total = None
        for at, s in zip(range(0, TK, TR), found):
            part = nn(vft[g, :, at : at + TR], jnp.exp2((s - top) * SCORE).astype(BF16))
            total = part if total is None else total + part
        return total

    def update(plans):
        scores = [[(g, scores_of(e, g, mask)) for g, mask in plan] for e, plan in enumerate(plans)]
        for e, plan in enumerate(scores):
            old, top = sums[e], tops[e]
            new = top
            for _, found in plan:
                for s in found:
                    new = jnp.maximum(new, jnp.max(s, axis=0, keepdims=True))
            total = old * jnp.exp2((top - new) * SCORE)
            for g, found in plan:
                total = total + mixed(g, found, new)
            sums[e] = total
            tops[e] = new

    def restart(top):
        for e in range(2):
            sums[e] = jnp.zeros((VROWS, TR), F32)
            tops[e] = top[e]

    lowest = jnp.full((1, TR), LOW, F32)

    @pl.when(i == 0)
    def _():
        restart((lowest, lowest))

    @pl.when(i > 0)
    def _():
        restart([jnp.max(nt(k_buf[0, :BLK, :], q_buf[e]), axis=0, keepdims=True) for e in range(2)])

        def quick(g, c):
            scores = [scores_of(e, g) for e in range(2)]
            totals = [sums[e] + mixed(g, scores[e], tops[e]) for e in range(2)]
            for e in range(2):
                sums[e] = totals[e]
            return c

        lax.fori_loop(0, a, quick, 0)
        row = slice(HD + FD, HD + FD + 1)
        largest = jnp.max(jnp.maximum(sums[0, row, :], sums[1, row, :]))

        @pl.when(jnp.logical_not(largest < SAFE))
        def _():
            restart((lowest, lowest))

            def slow(g, c):
                update([[(g, None)]] * 2)
                return c

            lax.fori_loop(0, a, slow, 0)

    tail_rows = jnp.where(iota((VROWS - HD - FD, TK), 0) == 0, 1.0, 0.0).astype(BF16)
    feats = []
    for e, g in enumerate((a, b)):
        parts = []
        for j, slab in enumerate(slabs):
            at = slice(j * BLK, (j + 1) * BLK)
            zh, x = column(where, j)
            part = jnp.concatenate(feats_of(slab, e, BLK), axis=0)
            parts.append(part)
            k_buf[g, at, :] = slab[e, :BLK, :]
            vft[g, :HD, at] = values[e, zh * 4 + x].T
            vft[g, HD : HD + FD, at] = part.T
        vft[g, HD + FD :, :] = tail_rows
        feats.append(jnp.concatenate(parts, axis=0))
    masks = [tile_mask(blocks, where, g, range(COLUMNS)) for g in (a, b)]
    update([[(a, masks[0])], [(a, None), (b, masks[1])]])
    for e, g in enumerate((a, b)):
        inv_n = FEAT_SCALE / (row_positions(blocks, where, g) + 1).astype(F32)
        student = jnp.where(masks[e], nt(feats[e], qf_buf[e]) * inv_n, 0.0).astype(BF16)
        state = prefix[...]
        high, low = split(state[:HD])
        linear = (nt(high, qf_buf[e]) + nt(low, qf_buf[e])) * inv_n
        pack[e, :HD, :] = sums[e, :HD, :]
        pack[e, HD : 2 * HD, :] = nn(vft[g, :HD, :], student) + linear
        pack[e, 2 * HD :, :] = jnp.where(iota((8, TR), 0) == 0, sums[e, HD + FD : HD + FD + 1, :], tops[e])
        okf[e] = sums[e, HD : HD + FD, :]
        states[e] = state.T
        prefix[...] = state + nn(vft[g, : HD + FD, :], feats[e])


def backward_kernel(blocks, where, own, other, values, *rest):
    slabs = rest[:COLUMNS]
    mine, theirs, okf, states, dk_out, dq_out = rest[COLUMNS : COLUMNS + 6]
    k_buf, vk_buf, kft, q_buf, qf_buf, rk_buf, bias, acc, state = rest[COLUMNS + 6 :]
    step = pl.program_id(0)
    i = PAIRS - 1 - step
    a, b = 2 * i, 2 * i + 1

    @pl.when(step == 0)
    def _():
        state[...] = jnp.zeros_like(state)

    for here, at in core_slices(where):
        ref = own if here else other
        for e, k in enumerate((a, b)):
            q_buf[k, at, :] = ref[e, :BLK, :]
            qf_buf[k, :, at] = jnp.concatenate([part.T for part in feats_of(ref, e, BLK)], axis=1)
    for e, k in enumerate((a, b)):
        l0, m0 = mine[e, 2 * HD : 2 * HD + 1, :], mine[e, 2 * HD + 1 : 2 * HD + 2, :]
        l1, m1 = theirs[e, 2 * HD : 2 * HD + 1, :], theirs[e, 2 * HD + 1 : 2 * HD + 2, :]
        top = jnp.maximum(m0, m1)
        w0, w1 = jnp.exp2((m0 - top) * SCORE), jnp.exp2((m1 - top) * SCORE)
        total = l0 * w0 + l1 * w1
        w0, w1 = w0 / total, w1 / total
        mixed = (mine[e, :HD, :] * w0 + theirs[e, :HD, :] * w1) - (
            mine[e, HD : 2 * HD, :] + theirs[e, HD : 2 * HD, :]
        )
        n = (row_positions(blocks, where, k) + 1).astype(F32)
        student = split(qf_buf[k].astype(F32) * (-FEAT_SCALE / (KEY_SCALE * jnp.sqrt(n))))
        rk_buf[e] = jnp.concatenate([mixed.astype(BF16), *student], axis=0)
        bias[k] = (0.5 * jnp.log2(n) - jnp.log2(total)) - top * SCORE
        dq_out[e] = okf[e] * (w0 * jnp.sqrt(n))
        for j, slab in enumerate(slabs):
            at = slice(j * BLK, (j + 1) * BLK)
            zh, x = column(where, j)
            feats = jnp.concatenate(feats_of(slab, e, BLK), axis=0)
            k_buf[e, at, :] = slab[e, :BLK, :]
            vk_buf[e, at, :] = jnp.concatenate([values[e, zh * 4 + x], feats, feats], axis=1)
            kft[e, :, at] = feats.T

    def teach(e, k):
        return nt(k_buf[e], q_buf[k]) * SCORE + bias[k]

    def diagonal(g, e):
        mask = tile_mask(blocks, where, g, range(COLUMNS))
        rk_tile, qf_tile, vk_tile = rk_buf[e], qf_buf[g], vk_buf[e]
        linear = jnp.where(mask, nn(vk_tile, rk_tile) * KEY_SCALE, 0.0)
        p = jnp.exp2(jnp.where(mask, teach(e, g), FLOOR))
        total = halves(nt(stacked(state[...]), vk_tile)) * KEY_SCALE
        total = total + nt(qf_tile, (p + linear).astype(BF16))
        if e == 0:
            p = jnp.exp2(teach(e, b)).astype(BF16)
            total = total + nt(qf_buf[b], p)
        acc[e] = total
        past = states[e]
        query = halves(nn(stacked(jnp.concatenate([past, past[:, HD:]], axis=1)), rk_tile)) * KEY_SCALE
        query = query + nn(kft[e], linear.astype(BF16))
        dq_out[e] = -(dq_out[e] + query)
        state[...] += nt(qf_tile, rk_tile)

    diagonal(b, 1)
    diagonal(a, 0)

    def full(t, c):
        olds = [acc[e] for e in range(2)]
        for e in range(2):
            p = [jnp.exp2(score).astype(BF16) for score in [teach(e, 2 * t), teach(e, 2 * t + 1)]]
            olds[e] = olds[e] + (nt(qf_buf[2 * t], p[0]) + nt(qf_buf[2 * t + 1], p[1]))
        for e in range(2):
            acc[e] = olds[e]
        return c

    lax.fori_loop(i + 1, PAIRS, full, 0)
    result = -jnp.concatenate([acc[0], acc[1]], axis=0).astype(dk_out.dtype)
    for j in range(COLUMNS):
        zh, x = column(where, j)
        dk_out[zh * 4 + x] = result[:, j * BLK : (j + 1) * BLK]


def smem(count):
    return [pl.BlockSpec(memory_space=pltpu.SMEM)] * count


def by_pair(rows, lanes, down=False):
    return pl.BlockSpec((2, rows, lanes), lambda s: (PAIRS - 1 - s if down else s, 0, 0))


def values_by_pair(down=False):
    return pl.BlockSpec((2, COLUMNS, BLK, HD), lambda s: (PAIRS - 1 - s if down else s, 0, 0, 0))


def forward(blocks, where, own, other, values, slabs):
    return pl.pallas_call(
        forward_kernel,
        grid=(PAIRS,),
        out_shape=(
            jax.ShapeDtypeStruct((GROUPS, PACK, TR), F32),
            jax.ShapeDtypeStruct((GROUPS, FD, TR), F32),
            jax.ShapeDtypeStruct((GROUPS, FD, HD + FD), F32),
        ),
        in_specs=smem(2) + [by_pair(PART, HD)] * 2 + [values_by_pair()] + [by_pair(PART, HD)] * COLUMNS,
        out_specs=[by_pair(PACK, TR), by_pair(FD, TR), by_pair(FD, HD + FD)],
        scratch_shapes=[
            pltpu.VMEM((GROUPS, TK, HD), BF16),
            pltpu.VMEM((GROUPS, VROWS, TK), BF16),
            pltpu.VMEM((2, TR, HD), BF16),
            pltpu.VMEM((2, TR, FD), BF16),
            pltpu.VMEM((2, VROWS, TR), F32),
            pltpu.VMEM((2, 1, TR), F32),
            pltpu.VMEM((HD + FD, FD), F32),
        ],
        cost_estimate=pl.CostEstimate(flops=20_000_000_000, transcendentals=9_400_000, bytes_accessed=16_000_000),
        name="forward",
    )(blocks, where, own, other, values, *slabs)


def backward(blocks, where, own, other, values, slabs, mine, theirs, okf, states):
    in_specs = smem(2) + [by_pair(PART, HD, True)] * 2 + [values_by_pair(True)]
    in_specs += [by_pair(PART, HD, True)] * COLUMNS
    in_specs += [by_pair(PACK, TR, True)] * 2 + [by_pair(FD, TR, True), by_pair(FD, HD + FD, True)]
    return pl.pallas_call(
        backward_kernel,
        grid=(PAIRS,),
        out_shape=(
            jax.ShapeDtypeStruct((COLUMNS, PAIRS * BLK, BLK), BF16),
            jax.ShapeDtypeStruct((GROUPS, FD, TR), F32),
        ),
        in_specs=in_specs,
        out_specs=[
            pl.BlockSpec((COLUMNS, BLK, BLK), lambda s: (0, PAIRS - 1 - s, 0)),
            by_pair(FD, TR, True),
        ],
        scratch_shapes=[
            pltpu.VMEM((2, TK, HD), BF16),
            pltpu.VMEM((2, TK, TR), BF16),
            pltpu.VMEM((2, FD, TK), BF16),
            pltpu.VMEM((GROUPS, TR, HD), BF16),
            pltpu.VMEM((GROUPS, FD, TR), BF16),
            pltpu.VMEM((2, TR, TR), BF16),
            pltpu.VMEM((GROUPS, 1, TR), F32),
            pltpu.VMEM((2, FD, TK), F32),
            pltpu.VMEM((FD, TR), F32),
        ],
        cost_estimate=pl.CostEstimate(flops=20_000_000_000, transcendentals=9_400_000, bytes_accessed=16_000_000),
        name="backward",
    )(blocks, where, own, other, values, *slabs, mine, theirs, okf, states)


def shifted(a, step):
    return lax.ppermute(a, "x", [(i, (i + step) % 4) for i in range(4)])


def across(a, axis):
    return lax.ppermute(a, axis, [(0, 1), (1, 0)])


def by_head(feats):
    return feats.reshape(2, HALF, GROUPS, FD).transpose(2, 1, 0, 3).reshape(GROUPS, HALF, 2 * FD)


def to_all(a, axes):
    return lax.all_to_all(jnp.broadcast_to(a[None], (8, *a.shape)), axes, 0, 0, tiled=True)


def per_device(queries, keys, values, query_feats, key_feats, block_pos):
    shared = jnp.broadcast_to(keys[None], (GROUPS, BLK, HD))
    slab = lax.all_to_all(jnp.concatenate([shared, by_head(key_feats)], axis=1), HEADS, 0, 0, tiled=True)
    left, right = shifted(slab, 1), shifted(slab, 3)
    far = across(slab, "zh")
    values = to_all(to_all(values, COLS), HEADS)
    q_heads = queries.reshape(BLK, GROUPS, HD).transpose(1, 0, 2)
    own = lax.all_to_all(jnp.concatenate([q_heads, by_head(query_feats)], axis=1), HEADS, 0, 0, tiled=True)
    other = across(own, "c")
    far_left, far_right = shifted(far, 1), shifted(far, 3)
    behind = jnp.concatenate([shifted(left[:4], 1), shifted(right[4:], 3)], axis=0)
    far_behind = jnp.concatenate([shifted(far_left[:4], 1), shifted(far_right[4:], 3)], axis=0)
    slabs = (slab, far, left, right, far_left, far_right, behind, far_behind)
    c = lax.axis_index("c")
    where = jnp.stack([lax.axis_index("zh"), lax.axis_index("x"), c]).astype(jnp.int32)

    mine, okf, states = forward(block_pos, where, own, other, values, slabs)
    theirs = across(mine, "c")
    dk, dq = backward(block_pos, where, own, other, values, slabs, mine, theirs, okf, states)

    dk = lax.all_to_all(dk, COLS, 0, 0, tiled=True).astype(F32).sum(axis=0)
    dq = dq.reshape(GROUPS, FD, 2, BLK)
    keep = lax.dynamic_slice_in_dim(dq, c, 1, 2)
    give = lax.dynamic_slice_in_dim(dq, 1 - c, 1, 2)
    dq = (keep + across(give, "c"))[:, :, 0]
    final = jnp.concatenate([dq, dk.reshape(GROUPS, FD, BLK)], axis=1)
    final = lax.all_to_all(final, HEADS, 0, 0, tiled=True)
    return final[:, :FD].reshape(-1, BLK).T, final[:, FD:].reshape(-1, BLK).T


def solution(mesh):
    split_mesh = Mesh(mesh.devices.reshape(2, 4, 2, 4, 2), ("zl", "y", "zh", "x", "c"))
    spec = P(("zl", "y", "zh", "x", "c"), None)
    return jax.shard_map(
        per_device,
        mesh=split_mesh,
        in_specs=(spec,) * 5 + (P(),),
        out_specs=(spec, spec),
        check_vma=False,
    )
```

```python
import functools
import math

import jax
import jax.numpy as jnp
from jax import lax
from jax.experimental import pallas as pl
from jax.experimental.pallas import tpu as pltpu
from jax.sharding import Mesh, PartitionSpec as P


FLOOR = -1e30
LOW = -1e29
F32 = jnp.float32
BF16 = jnp.bfloat16
HEADS = ("zl", "y")
COLS = ("zh", "x")
BLK = 128
GROUPS = 8
COLUMNS = 8
HD = 128
FD = 64
TR = 2 * BLK
TK = COLUMNS * BLK
PAIRS = GROUPS // 2
HALF = BLK // 2
WIDTH = 4
KEYS = WIDTH * BLK
SAFE = 2.0**100
SLAB = 2 * BLK + HALF
ROWS = BLK + HALF
VROWS = 208
ROW_L = VROWS
ROW_M = VROWS + HD
CARRY = ROW_M + 8
PACK = 2 * HD + 8
PLACES = ((0, 0), (1, 0), (0, 3), (0, 1), (1, 3), (1, 1), (0, 2), (1, 2))
KEY_SCALE = 1.0 / math.sqrt(HD)
FEAT_SCALE = 1.0 / math.sqrt(FD)
SCORE = KEY_SCALE * math.log2(math.e)


def nn(a, b):
    return lax.dot_general(a, b, (((1,), (0,)), ((), ())), preferred_element_type=F32)


def nt(a, b):
    return lax.dot_general(a, b, (((1,), (1,)), ((), ())), preferred_element_type=F32)


def split(a):
    high = a.astype(BF16)
    return high, (a - high.astype(F32)).astype(BF16)


def stacked(a):
    return jnp.concatenate(split(a), axis=0)


def halves(a):
    return a[: a.shape[0] // 2] + a[a.shape[0] // 2 :]


def iota(shape, dim):
    return lax.broadcasted_iota(jnp.int32, shape, dim)


def column(where, j):
    zh, x = PLACES[j]
    return (where[0] + zh) % 2, (where[1] + x) % 4


def row_positions(blocks, where, k):
    lane = iota((1, TR), 1)
    at = k * 16 + where[0] * 8 + where[1] * 2
    first = blocks[at] * BLK
    second = blocks[at + 1] * BLK - BLK
    return lane + jnp.where(lane < BLK, first, second)


def tile_mask(blocks, where, k, columns):
    pos_rows = row_positions(blocks, where, k)
    step = iota((BLK, 1), 0)
    parts = []
    for j in columns:
        zh, x = column(where, j)
        parts.append(pos_rows >= step + blocks[k * 16 + zh * 8 + x * 2 + where[2]] * BLK)
    return jnp.concatenate(parts, axis=0)


def feats_of(ref, e, at):
    packed = ref[e, at : at + HALF, :]
    return packed[:, :FD], packed[:, FD:]


def core_slices(where):
    for mine, slot in ((True, where[2]), (False, 1 - where[2])):
        yield mine, pl.ds(pl.multiple_of(slot * BLK, BLK), BLK)


def forward_kernel(columns, first, last, *refs):
    blocks, where, own, other = refs[:4]
    slabs = refs[4 : 4 + WIDTH]
    refs = refs[4 + WIDTH :]
    if not first:
        carry_in, sums_in = refs[:2]
        refs = refs[2:]
    if last:
        pack, okf, states = refs[:3]
        carry, prefix = refs[3:5]
        refs = refs[5:]
    else:
        carry, sums = refs[:2]
        refs = refs[2:]
    k_buf, vft, q_buf, qf_buf = refs
    i = pl.program_id(0)
    a, b = 2 * i, 2 * i + 1
    if last:

        @pl.when(i == 0)
        def _():
            prefix[...] = jnp.zeros_like(prefix)

    for mine, at in core_slices(where):
        ref = own if mine else other
        for e in range(2):
            q_buf[e, at, :] = ref[e, :BLK, :]
            qf_buf[e, at, :] = jnp.concatenate(feats_of(ref, e, BLK), axis=0)

    def scores_of(e, g, mask=None):
        found = []
        for at in range(0, KEYS, TR):
            s = nt(k_buf[g, at : at + TR, :], q_buf[e])
            found.append(s if mask is None else jnp.where(mask[at : at + TR], s, FLOOR))
        return found

    def added(total, g, found, top):
        for at, s in zip(range(0, KEYS, TR), found):
            total = total + nn(vft[g, :, at : at + TR], jnp.exp2((s - top) * SCORE).astype(BF16))
        return total

    def update(plans):
        scores = [[(g, scores_of(e, g, mask)) for g, mask in plan] for e, plan in enumerate(plans)]
        for e, plan in enumerate(scores):
            top = carry[e, ROW_M : ROW_M + 1, :]
            new = top
            for _, found in plan:
                for s in found:
                    new = jnp.maximum(new, jnp.max(s, axis=0, keepdims=True))
            total = carry[e, :VROWS, :] * jnp.exp2((top - new) * SCORE)
            for g, found in plan:
                total = added(total, g, found, new)
            carry[e, :VROWS, :] = total
            carry[e, ROW_M : ROW_M + 1, :] = new

    def restart():
        for e in range(2):
            if first:
                carry[e, :VROWS, :] = jnp.zeros((VROWS, TR), F32)
                carry[e, ROW_M : ROW_M + 1, :] = jnp.full((1, TR), LOW, F32)
            else:
                carry[e, :VROWS, :] = carry_in[e, :VROWS, :]
                carry[e, ROW_M : ROW_M + 1, :] = carry_in[e, ROW_M : ROW_M + 1, :]

    restart()

    @pl.when(i > 0)
    def _():
        if first:
            for e in range(2):
                s = nt(k_buf[0, :BLK, :], q_buf[e])
                carry[e, ROW_M : ROW_M + 1, :] = jnp.max(s, axis=0, keepdims=True)

        def quick(u, c):
            scores = [[scores_of(e, 2 * u + d) for d in range(2)] for e in range(2)]
            totals = []
            for e in range(2):
                top = carry[e, ROW_M : ROW_M + 1, :]
                total = carry[e, :VROWS, :]
                for d in range(2):
                    total = added(total, 2 * u + d, scores[e][d], top)
                totals.append(total)
            for e in range(2):
                carry[e, :VROWS, :] = totals[e]
            return c

        lax.fori_loop(0, i, quick, 0)
        row = slice(HD + FD, HD + FD + 1)
        largest = jnp.max(jnp.maximum(carry[0, row, :], carry[1, row, :]))

        @pl.when(jnp.logical_not(largest < SAFE))
        def _():
            restart()

            def slow(g, c):
                update([[(g, None)]] * 2)
                return c

            lax.fori_loop(0, a, slow, 0)

    tail_rows = jnp.where(iota((VROWS - HD - FD, KEYS), 0) == 0, 1.0, 0.0).astype(BF16)
    feats = []
    for e, g in enumerate((a, b)):
        parts = []
        for j, slab in enumerate(slabs):
            at = slice(j * BLK, (j + 1) * BLK)
            part = jnp.concatenate(feats_of(slab, e, 2 * BLK), axis=0)
            parts.append(part)
            k_buf[g, at, :] = slab[e, :BLK, :]
            vft[g, :HD, at] = slab[e, BLK : 2 * BLK, :].T
            vft[g, HD : HD + FD, at] = part.T
        vft[g, HD + FD :, :] = tail_rows
        feats.append(jnp.concatenate(parts, axis=0))
    masks = [tile_mask(blocks, where, g, columns) for g in (a, b)]
    update([[(a, masks[0])], [(a, None), (b, masks[1])]])
    for e, g in enumerate((a, b)):
        inv_n = FEAT_SCALE / (row_positions(blocks, where, g) + 1).astype(F32)
        student = jnp.where(masks[e], nt(feats[e], qf_buf[e]) * inv_n, 0.0).astype(BF16)
        linear = nn(vft[g, :HD, :], student)
        moment = nn(vft[g, : HD + FD, :], feats[e])
        if not first:
            linear = linear + carry_in[e, ROW_L:ROW_M, :]
            moment = moment + sums_in[e]
        if not last:
            carry[e, ROW_L:ROW_M, :] = linear
            sums[e] = moment
        else:
            state = prefix[...]
            high, low = split(state[:HD])
            pack[e, :HD, :] = carry[e, :HD, :]
            pack[e, HD : 2 * HD, :] = linear + (nt(high, qf_buf[e]) + nt(low, qf_buf[e])) * inv_n
            norm = carry[e, HD + FD : HD + FD + 1, :]
            top = carry[e, ROW_M : ROW_M + 1, :]
            pack[e, 2 * HD :, :] = jnp.where(iota((8, TR), 0) == 0, norm, top)
            okf[e] = carry[e, HD : HD + FD, :]
            states[e] = state.T
            prefix[...] = state + moment


def backward_kernel(blocks, where, own, other, *rest):
    slabs = rest[:COLUMNS]
    mine, theirs, okf, states, dk_out, dq_out = rest[COLUMNS : COLUMNS + 6]
    k_buf, vk_buf, kft, q_buf, qf_buf, rk_buf, bias, acc, state = rest[COLUMNS + 6 :]
    step = pl.program_id(0)
    i = PAIRS - 1 - step
    a, b = 2 * i, 2 * i + 1

    @pl.when(step == 0)
    def _():
        state[...] = jnp.zeros_like(state)

    for here, at in core_slices(where):
        ref = own if here else other
        for e, k in enumerate((a, b)):
            q_buf[k, at, :] = ref[e, :BLK, :]
            qf_buf[k, :, at] = jnp.concatenate([part.T for part in feats_of(ref, e, BLK)], axis=1)
    for e, k in enumerate((a, b)):
        l0, m0 = mine[e, 2 * HD : 2 * HD + 1, :], mine[e, 2 * HD + 1 : 2 * HD + 2, :]
        l1, m1 = theirs[e, 2 * HD : 2 * HD + 1, :], theirs[e, 2 * HD + 1 : 2 * HD + 2, :]
        top = jnp.maximum(m0, m1)
        w0, w1 = jnp.exp2((m0 - top) * SCORE), jnp.exp2((m1 - top) * SCORE)
        total = l0 * w0 + l1 * w1
        w0, w1 = w0 / total, w1 / total
        mixed = (mine[e, :HD, :] * w0 + theirs[e, :HD, :] * w1) - (
            mine[e, HD : 2 * HD, :] + theirs[e, HD : 2 * HD, :]
        )
        n = (row_positions(blocks, where, k) + 1).astype(F32)
        student = split(qf_buf[k].astype(F32) * (-FEAT_SCALE / (KEY_SCALE * jnp.sqrt(n))))
        rk_buf[e] = jnp.concatenate([mixed.astype(BF16), *student], axis=0)
        bias[k] = (0.5 * jnp.log2(n) - jnp.log2(total)) - top * SCORE
        dq_out[e] = okf[e] * (w0 * jnp.sqrt(n))
        for j, slab in enumerate(slabs):
            at = slice(j * BLK, (j + 1) * BLK)
            feats = jnp.concatenate(feats_of(slab, e, 2 * BLK), axis=0)
            k_buf[e, at, :] = slab[e, :BLK, :]
            vk_buf[e, at, :] = jnp.concatenate([slab[e, BLK : 2 * BLK, :], feats, feats], axis=1)
            kft[e, :, at] = feats.T

    def teach(e, k):
        return nt(k_buf[e], q_buf[k]) * SCORE + bias[k]

    def diagonal(g, e):
        mask = tile_mask(blocks, where, g, range(COLUMNS))
        rk_tile, qf_tile, vk_tile = rk_buf[e], qf_buf[g], vk_buf[e]
        linear = jnp.where(mask, nn(vk_tile, rk_tile) * KEY_SCALE, 0.0)
        p = jnp.exp2(jnp.where(mask, teach(e, g), FLOOR))
        total = halves(nt(stacked(state[...]), vk_tile)) * KEY_SCALE
        total = total + nt(qf_tile, (p + linear).astype(BF16))
        if e == 0:
            p = jnp.exp2(teach(e, b)).astype(BF16)
            total = total + nt(qf_buf[b], p)
        acc[e] = total
        past = states[e]
        query = halves(nn(stacked(jnp.concatenate([past, past[:, HD:]], axis=1)), rk_tile)) * KEY_SCALE
        query = query + nn(kft[e], linear.astype(BF16))
        dq_out[e] = -(dq_out[e] + query)
        state[...] += nt(qf_tile, rk_tile)

    diagonal(b, 1)
    diagonal(a, 0)

    def full(t, c):
        olds = [acc[e] for e in range(2)]
        for e in range(2):
            p = [jnp.exp2(score).astype(BF16) for score in [teach(e, 2 * t), teach(e, 2 * t + 1)]]
            olds[e] = olds[e] + (nt(qf_buf[2 * t], p[0]) + nt(qf_buf[2 * t + 1], p[1]))
        for e in range(2):
            acc[e] = olds[e]
        return c

    lax.fori_loop(i + 1, PAIRS, full, 0)
    result = -jnp.concatenate([acc[0], acc[1]], axis=0).astype(dk_out.dtype)
    for j in range(COLUMNS):
        zh, x = column(where, j)
        dk_out[zh * 4 + x] = result[:, j * BLK : (j + 1) * BLK]


def smem(count):
    return [pl.BlockSpec(memory_space=pltpu.SMEM)] * count


def by_pair(rows, lanes, down=False):
    return pl.BlockSpec((2, rows, lanes), lambda s: (PAIRS - 1 - s if down else s, 0, 0))


def forward(columns, blocks, where, own, other, slabs, carried, last):
    carry = ((GROUPS, CARRY, TR), F32)
    sums = ((GROUPS, HD + FD, FD), F32)
    carry_specs = [by_pair(CARRY, TR), by_pair(HD + FD, FD)]
    if last:
        outs = [((GROUPS, PACK, TR), F32), ((GROUPS, FD, TR), F32), ((GROUPS, FD, HD + FD), F32)]
        out_specs = [by_pair(PACK, TR), by_pair(FD, TR), by_pair(FD, HD + FD)]
        scratch = [pltpu.VMEM((2, CARRY, TR), F32), pltpu.VMEM((HD + FD, FD), F32)]
    else:
        outs, out_specs, scratch = [carry, sums], carry_specs, []
    scratch += [
        pltpu.VMEM((GROUPS, KEYS, HD), BF16),
        pltpu.VMEM((GROUPS, VROWS, KEYS), BF16),
        pltpu.VMEM((2, TR, HD), BF16),
        pltpu.VMEM((2, TR, FD), BF16),
    ]
    in_specs = smem(2) + [by_pair(ROWS, HD)] * 2 + [by_pair(SLAB, HD)] * WIDTH
    return pl.pallas_call(
        functools.partial(forward_kernel, columns, not carried, last),
        grid=(PAIRS,),
        out_shape=tuple(jax.ShapeDtypeStruct(*o) for o in outs),
        in_specs=in_specs + (carry_specs if carried else []),
        out_specs=out_specs,
        scratch_shapes=scratch,
        cost_estimate=pl.CostEstimate(flops=6_000_000_000, transcendentals=2_400_000, bytes_accessed=8_000_000),
    )(blocks, where, own, other, *slabs, *carried)


def backward(blocks, where, own, other, slabs, mine, theirs, okf, states):
    in_specs = smem(2) + [by_pair(ROWS, HD, True)] * 2 + [by_pair(SLAB, HD, True)] * COLUMNS
    in_specs += [by_pair(PACK, TR, True)] * 2 + [by_pair(FD, TR, True), by_pair(FD, HD + FD, True)]
    return pl.pallas_call(
        backward_kernel,
        grid=(PAIRS,),
        out_shape=(
            jax.ShapeDtypeStruct((COLUMNS, PAIRS * BLK, BLK), BF16),
            jax.ShapeDtypeStruct((GROUPS, FD, TR), F32),
        ),
        in_specs=in_specs,
        out_specs=[
            pl.BlockSpec((COLUMNS, BLK, BLK), lambda s: (0, PAIRS - 1 - s, 0)),
            by_pair(FD, TR, True),
        ],
        scratch_shapes=[
            pltpu.VMEM((2, TK, HD), BF16),
            pltpu.VMEM((2, TK, TR), BF16),
            pltpu.VMEM((2, FD, TK), BF16),
            pltpu.VMEM((GROUPS, TR, HD), BF16),
            pltpu.VMEM((GROUPS, FD, TR), BF16),
            pltpu.VMEM((2, TR, TR), BF16),
            pltpu.VMEM((GROUPS, 1, TR), F32),
            pltpu.VMEM((2, FD, TK), F32),
            pltpu.VMEM((FD, TR), F32),
        ],
        cost_estimate=pl.CostEstimate(flops=20_000_000_000, transcendentals=9_400_000, bytes_accessed=16_000_000),
        name="backward",
    )(blocks, where, own, other, *slabs, mine, theirs, okf, states)


def shifted(a, step):
    return lax.ppermute(a, "x", [(i, (i + step) % 4) for i in range(4)])


def across(a, axis):
    return lax.ppermute(a, axis, [(0, 1), (1, 0)])


def by_head(feats):
    return feats.reshape(2, HALF, GROUPS, FD).transpose(2, 1, 0, 3).reshape(GROUPS, HALF, 2 * FD)


def step(queries, keys, values, query_feats, key_feats, block_pos):
    shared = jnp.broadcast_to(jnp.concatenate([keys, values], axis=0)[None], (GROUPS, 2 * BLK, HD))
    slab = lax.all_to_all(jnp.concatenate([shared, by_head(key_feats)], axis=1), HEADS, 0, 0, tiled=True)
    left = shifted(slab, 1)
    right = shifted(slab, 3)
    far = across(slab, "zh")
    q_heads = queries.reshape(BLK, GROUPS, HD).transpose(1, 0, 2)
    rows = jnp.concatenate([q_heads, by_head(query_feats)], axis=1)
    own = lax.all_to_all(rows, HEADS, 0, 0, tiled=True)
    other = across(own, "c")
    far_left, far_right = shifted(far, 1), shifted(far, 3)
    behind = jnp.concatenate([shifted(left[:4], 1), shifted(right[4:], 3)], axis=0)
    c = lax.axis_index("c")
    where = jnp.stack([lax.axis_index("zh"), lax.axis_index("x"), c]).astype(jnp.int32)

    carried = forward((0, 1, 2, 3), block_pos, where, own, other, (slab, far, left, right), (), False)
    far_left, far_right, *carried = lax.optimization_barrier((far_left, far_right, *carried))
    far_behind = jnp.concatenate([shifted(far_left[:4], 1), shifted(far_right[4:], 3)], axis=0)
    slabs = (slab, far, left, right, far_left, far_right, behind, far_behind)
    mine, okf, states = forward((4, 5, 6, 7), block_pos, where, own, other, slabs[4:], carried, True)
    theirs = across(mine, "c")
    dk, dq = backward(block_pos, where, own, other, slabs, mine, theirs, okf, states)

    dk = lax.all_to_all(dk, COLS, 0, 0, tiled=True).astype(F32).sum(axis=0)
    dq = dq.reshape(GROUPS, FD, 2, BLK)
    keep = lax.dynamic_slice_in_dim(dq, c, 1, 2)
    give = lax.dynamic_slice_in_dim(dq, 1 - c, 1, 2)
    dq = (keep + across(give, "c"))[:, :, 0]
    final = jnp.concatenate([dq, dk.reshape(GROUPS, FD, BLK)], axis=1)
    final = lax.all_to_all(final, HEADS, 0, 0, tiled=True)
    return final[:, :FD].reshape(-1, BLK).T, final[:, FD:].reshape(-1, BLK).T


def solution(mesh):
    split_mesh = Mesh(mesh.devices.reshape(2, 4, 2, 4, 2), ("zl", "y", "zh", "x", "c"))
    spec = P(("zl", "y", "zh", "x", "c"), None)
    return jax.shard_map(
        step,
        mesh=split_mesh,
        in_specs=(spec,) * 5 + (P(),),
        out_specs=(spec, spec),
        check_vma=False,
    )
```
